32 devices in a mesh: pipe: 4 (over x, core), expert: 8 (over z, y).
Axes of the slice: x: 2, y: 2, z: 4, core: 2. Of those that a mesh axis runs over, the one named last changes fastest.
Arguments:
- activations: bfloat16 [4, 2, 512, 7168], P('pipe', None, 'expert'), may hold values from -6 to 6
- expert_ids: int32 [4, 2, 512], P('pipe', None, 'expert'), may hold values from 0 to 1, as said below
- gate_values: float32 [4, 2, 512], P('pipe', None, 'expert'), may hold values from 0.5 to 1.5
- norm_gain: bfloat16 [4, 7168], P('pipe'), may hold values from 0.25 to 1.75
- up_weight: bfloat16 [4, 7168, 2048], P('pipe', None, 'expert'), may hold values from -0.0625 to 0.0625
- down_weight: bfloat16 [4, 2048, 7168], P('pipe', 'expert'), may hold values from -0.1875 to 0.1875
Outputs:
- received: bfloat16 [4, 2, 512, 7168], P('pipe', None, 'expert')
The draws below stay inside these ranges and needn't reach their ends.
Inputs may be any that keep to these rules, and one draw needn't show every extreme that they name: `expert_ids`: the 64 tokens of one device in one section and micro-batch (aligned blocks along the last dimension) name no expert more than 48 times; in every section and micro-batch one expert is named exactly 48 times by the tokens of every device.
All inputs are finite; a program needn't handle non-finite values.
Results may differ from the reference program's by a relative error of at most 0.0058.
Values may be sent and summed in bfloat16 or wider, within the bound.
A program may use at most 128 MiB of HBM per device.

```python
import jax
import jax.numpy as jnp
from jax import lax

D = 7168
FF_DEV = 256
TOK = 64
MB = 2
GROUP = 4
FF = 1024
EXPERTS = 2
CAP = 48
SECTIONS = 4
TOKENS = 512
N_EXPERT = 8


def one_block(block_key, hot_expert):
    pool_key, order_key = jax.random.split(block_key)
    others = jnp.arange((EXPERTS - 1) * CAP, dtype=jnp.int32) // CAP
    others = others + (others >= hot_expert).astype(jnp.int32)
    chosen = jax.random.permutation(pool_key, others)[:TOK - CAP]
    merged = jnp.concatenate([jnp.full((CAP,), hot_expert, jnp.int32), chosen])
    return jax.random.permutation(order_key, merged)


def draw_expert_ids(key, part):
    hot_key, block_key = jax.random.split(jax.random.fold_in(key, 17))
    hot_expert = jax.random.randint(hot_key, (SECTIONS * MB,), 0, EXPERTS, dtype=jnp.int32)
    block_keys = jax.random.split(block_key, SECTIONS * MB * N_EXPERT)
    hot_rows = jnp.repeat(hot_expert, N_EXPERT)
    blocks = jax.vmap(one_block)(block_keys, hot_rows)
    return blocks.reshape(SECTIONS, MB, N_EXPERT * TOK).astype(jnp.int32)


def shard_levels(key, dims, cuts, low, largest):
    def one(position, blocks):
        steps = jax.random.uniform(jax.random.fold_in(jax.random.fold_in(key, 6), position), (blocks,), jnp.float32, low / len(cuts), largest / len(cuts))
        return jnp.repeat(jnp.exp(steps), dims[position] // blocks).reshape((-1,) + (1,) * (len(dims) - position - 1))

    factor_of = one(*cuts[0])
    for cut in cuts[1:]:
        factor_of = factor_of * one(*cut)
    return factor_of


def noise(own_key, shape, deviation, bound, cuts=(), kind=jnp.bfloat16):
    values = deviation * jax.random.normal(own_key, shape, jnp.float32)
    if cuts:
        values = values * shard_levels(own_key, shape, cuts, -0.22, 0.18)
    return jnp.clip(values, -bound, bound).astype(kind)


def setup_inputs(seed: int = 0) -> dict:
    key_list = jax.random.split(jax.random.key(seed), 7)
    return {
        "activations": noise(key_list[0], (SECTIONS, MB, TOKENS, D), 1.0, 6.0, ((0, 4), (2, 8))),
        "expert_ids": draw_expert_ids(jax.random.fold_in(key_list[6], 71), 0),
        "gate_values": jnp.clip(0.5 + 1.0 * jax.random.uniform(key_list[2], (SECTIONS, MB, TOKENS), jnp.float32) ** shard_levels(key_list[2], (SECTIONS, MB, TOKENS), ((0, 4), (2, 8)), -0.2, 0.2), 0.5, 1.5),
        "norm_gain": jnp.clip(1.0 + 0.15 * jax.random.normal(key_list[3], (SECTIONS, D), jnp.float32), 0.25, 1.75).astype(jnp.bfloat16),
        "up_weight": noise(key_list[4], (SECTIONS, D, EXPERTS * FF), D ** -0.5, 0.0625, ((0, 4), (2, 8))),
        "down_weight": noise(key_list[5], (SECTIONS, EXPERTS * FF, D), FF ** -0.5, 0.1875, ((0, 4), (1, 8))),
    }


EPSILON = 1e-06

def section_layer(activations, expert_ids, gate_values, norm_gain, up_weight, down_weight):
    widened = activations.astype(jnp.float32)
    scale_inv = lax.rsqrt(lax.optimization_barrier(jnp.mean(widened * widened, axis=-1, keepdims=True)) + EPSILON)
    normed = (widened * scale_inv * norm_gain.astype(jnp.float32)).astype(jnp.bfloat16)
    onehot = (expert_ids[:, None] == jnp.arange(EXPERTS, dtype=jnp.int32)[None, :]).astype(jnp.int32)
    blocked = onehot.reshape(N_EXPERT, TOK, EXPERTS)
    before = jnp.cumsum(blocked, axis=1) - blocked
    ranking = lax.optimization_barrier(jnp.sum(before * blocked, axis=-1)).reshape(TOKENS).astype(jnp.int32)
    source = jnp.arange(TOKENS, dtype=jnp.int32) // TOK
    slot_index = (source * CAP + ranking).astype(jnp.int32)
    buffers = jnp.zeros((EXPERTS, N_EXPERT * CAP, D), jnp.bfloat16).at[expert_ids, slot_index].set(normed)
    up_experts = up_weight.reshape(D, EXPERTS, FF).transpose(1, 0, 2)
    down_experts = down_weight.reshape(EXPERTS, GROUP, FF_DEV, D)
    half_group = GROUP // 2

    def one_expert(packed):
        arriving, up_one, down_one = packed
        hidden = jax.nn.silu(jnp.dot(arriving, up_one, preferred_element_type=jnp.float32)).astype(jnp.bfloat16)
        pieces = hidden.reshape(arriving.shape[0], GROUP, FF_DEV)
        partials = jnp.einsum('rgf,gfd->grd', pieces.astype(jnp.float32), down_one.astype(jnp.float32)).astype(jnp.bfloat16)
        widened_parts = partials.astype(jnp.float32)
        pairs = (widened_parts[:half_group] + widened_parts[half_group:]).astype(jnp.bfloat16)
        pairs = lax.optimization_barrier(pairs)
        return lax.optimization_barrier(jnp.sum(pairs.astype(jnp.float32), axis=0)).astype(jnp.bfloat16)
    results = lax.map(one_expert, (buffers, up_experts, down_experts))
    expert_out = results[expert_ids, slot_index]
    return (widened + gate_values.astype(jnp.float32)[:, None] * expert_out.astype(jnp.float32)).astype(jnp.bfloat16)

def reference(activations, expert_ids, gate_values, norm_gain, up_weight, down_weight):
    section_outputs = []
    for section_index in range(SECTIONS):
        batch_outputs = []
        for batch_index in range(MB):
            batch_outputs.append(section_layer(activations[section_index, batch_index], expert_ids[section_index, batch_index], gate_values[section_index, batch_index], norm_gain[section_index], up_weight[section_index], down_weight[section_index]))
        section_outputs.append(jnp.stack(batch_outputs))
    layer_out = jnp.stack(section_outputs)
    return jnp.roll(layer_out, 1, axis=0)
```

```python
import functools

import jax
import jax.numpy as jnp
from jax import lax
from jax.experimental import pallas as pl
from jax.experimental.pallas import tpu as pltpu
from jax.sharding import PartitionSpec as P

LEVELS = 2


EPSILON = 1e-06
GROUP = 2**LEVELS
MESH = pl.DeviceIdType.MESH
F32, BF16 = jnp.float32, jnp.bfloat16


def remote(source, target, send, recv, **where):
    return pltpu.make_async_remote_copy(
        src_ref=source, dst_ref=target, send_sem=send, recv_sem=recv, device_id=where, device_id_type=MESH
    )


def each(low, high, body):
    def step(index, carry):
        body(index)
        return carry

    lax.fori_loop(low, high, step, 0)


def layer_kernel(
    n, pipes, place, act, gain, gate, up, down, ret, act_out, place_out, gate_out,
    packed, x, up_all, down_all, pres, sums, own_pre, hidden, out,
    usend, urecv, dsend, drecv, psend, precv, xsend, xrecv, ssend, srecv, hsend, hrecv, rsend, rrecv, own,
):
    me, pipe = lax.axis_index("expert"), lax.axis_index("pipe")
    group_index = me // GROUP
    first = group_index * GROUP
    g = me - first
    batches, experts, capacity = place.shape[:3]
    part, units = up.shape[1:]
    ahead, behind = (pipe + 1) % pipes, (pipe + pipes - 1) % pipes
    blocks = n // GROUP
    tall = GROUP * capacity

    barrier = pltpu.get_barrier_semaphore()

    def greet(k):
        pl.semaphore_signal(barrier, inc=1, device_id={"expert": (me + k) % n}, device_id_type=MESH)

    def greet_behind(k):
        pl.semaphore_signal(barrier, inc=1, device_id={"pipe": behind, "expert": k}, device_id_type=MESH)

    each(1, n, greet)
    each(0, n, greet_behind)
    pl.semaphore_wait(barrier, 2 * n - 1)

    def columns(j):
        return pl.ds(pl.multiple_of(j * part, 128), part)

    def share(j):
        return pl.ds(pl.multiple_of(j * units, 128), units)

    def rows_of(d):
        return pl.ds(pl.multiple_of(d * capacity, 16), capacity)

    peers = [(k, (g + k) % GROUP) for k in range(1, GROUP)]
    ups = [remote(up.at[j], up_all.at[g], usend.at[k], urecv.at[k], expert=first + j) for k, j in peers]
    downs = [
        remote(
            down.at[:, columns(j)], down_all.at[share(g), :], dsend.at[k], drecv.at[k], expert=first + j
        )
        for k, j in peers
    ]
    shifts = [
        remote(source, target, psend.at[i], precv.at[i], pipe=ahead)
        for i, (source, target) in enumerate(((act, act_out), (place, place_out), (gate, gate_out)))
    ]

    def dispatch(m, k):
        d = (me + k) % n
        return remote(packed.at[m, d], x.at[m, rows_of(me), :], xsend.at[m, k], xrecv.at[m, k], expert=d)

    for copy in ups:
        copy.start()
    own_up = pltpu.make_async_copy(up.at[g], up_all.at[g], own.at[0])
    own_down = pltpu.make_async_copy(down.at[:, columns(g)], down_all.at[share(g), :], own.at[1])
    own_up.start()
    own_down.start()
    own_rows = []
    for m in range(batches):
        wide = act[m].astype(F32)
        scale = lax.rsqrt(jnp.mean(wide * wide, axis=-1, keepdims=True) + EPSILON)
        normed = (wide * scale * gain[...].astype(F32)).astype(BF16)
        for e in range(experts):
            for j in range(GROUP):
                packed[m, e * GROUP + j] = jnp.dot(
                    place[m, e], normed[:, j * part : (j + 1) * part], preferred_element_type=F32
                ).astype(BF16)
        if m == 0:
            each(1, n, lambda k: dispatch(0, k).start())
        copy = pltpu.make_async_copy(packed.at[m, me], x.at[m, rows_of(me), :], own.at[2 + m])
        copy.start()
        own_rows.append(copy)

    def summing(m, k, j):
        return remote(pres.at[m, k], sums.at[m, k], ssend.at[m, k], srecv.at[m, k], expert=first + j)

    def sharing(m, k, j):
        mine = hidden.at[m, :, share(g)]
        return remote(mine, mine, hsend.at[m, k], hrecv.at[m, k], expert=first + j)

    own_up.wait()
    for copy in ups:
        copy.wait_recv()
    for m in range(batches):
        own_rows[m].wait()
        each(1, n, lambda k, m=m: dispatch(m, k).wait_recv())
        for k, j in peers:
            pres[m, k] = jnp.dot(x[m], up_all[j], preferred_element_type=F32).astype(BF16)
            summing(m, k, j).start()
        if m + 1 < batches:
            each(1, n, lambda k, m=m: dispatch(m + 1, k).start())
        if m == 0:
            for copy in downs + shifts:
                copy.start()
        own_pre[...] = jnp.dot(x[m], up_all[g], preferred_element_type=F32)
        for k, j in peers:
            summing(m, k, j).wait_recv()
        total = own_pre[...]
        for k in range(1, GROUP):
            total = total + sums[m, k].astype(F32)
        hidden[m, :, share(g)] = jax.nn.silu(total).astype(BF16)
        for k, j in peers:
            sharing(m, k, j).start()

    def slots_of(m, source):
        return ret.at[m, rows_of(source // GROUP), columns(source % GROUP)]

    def give(m, target):
        return remote(
            out.at[m, rows_of(target), :], slots_of(m, me), rsend.at[m, target], rrecv.at[m, me],
            pipe=ahead, expert=target,
        )

    own_down.wait()
    for copy in downs:
        copy.wait_recv()
    for m in range(batches):
        for k, j in peers:
            sharing(m, k, j).wait_recv()

        def block(index, m=m):
            owner = (group_index + 1 + index) % blocks
            rows = pl.ds(pl.multiple_of(owner * tall, 16), tall)
            out[m, rows, :] = jnp.dot(
                hidden[m, rows, :], down_all[...], preferred_element_type=F32
            ).astype(BF16)
            for j in range(GROUP):
                give(m, owner * GROUP + j).start()

        each(0, blocks, block)

    for copy in ups + downs:
        copy.wait_send()
    for copy in shifts:
        copy.wait()
    for m in range(batches):
        each(1, n, lambda k, m=m: dispatch(m, k).wait_send())
        for k, j in peers:
            summing(m, k, j).wait_send()
            sharing(m, k, j).wait_send()

        def finish(source, m=m):
            give(m, source).wait_send()
            remote(
                out.at[m, rows_of(source), :], slots_of(m, source), rsend.at[m, source],
                rrecv.at[m, source], pipe=ahead, expert=source,
            ).wait_recv()

        each(0, n, finish)


def general(pipes, activations, expert_ids, gate_values, norm_gain, up_weight, down_weight):
    n = lax.axis_size("expert")
    experts = n // GROUP
    _, batches, tok, width = activations.shape
    part = width // GROUP
    units = up_weight.shape[2]
    capacity = max(2, 3 * tok // (2 * experts))
    capacity = (capacity + 15) // 16 * 16
    rows = n * capacity

    order = jnp.arange(tok, dtype=jnp.int32)
    same = expert_ids[0][:, :, None] == expert_ids[0][:, None, :]
    ranking = jnp.sum((same & (order[None, :] < order[:, None])).astype(jnp.int32), axis=-1)
    slot = expert_ids[0] * capacity + ranking
    slots = jnp.arange(experts * capacity, dtype=jnp.int32).reshape(1, experts, capacity, 1)
    place = (slot[:, None, None, :] == slots).astype(BF16)

    vmem, far = pl.BlockSpec(memory_space=pltpu.VMEM), pl.BlockSpec(memory_space=pl.ANY)
    shape, sem = jax.ShapeDtypeStruct, pltpu.SemaphoreType.DMA
    returned, act_prev, place_prev, gate_prev = pl.pallas_call(
        functools.partial(layer_kernel, n, pipes),
        out_shape=(
            shape((batches, experts * capacity, width), BF16),
            shape((batches, tok, width), BF16),
            shape(place.shape, BF16),
            shape((batches, tok), F32),
        ),
        in_specs=[vmem] * 4 + [far] * 2,
        out_specs=(far,) * 4,
        scratch_shapes=[
            pltpu.VMEM((batches, n, capacity, part), BF16),
            pltpu.VMEM((batches, rows, part), BF16),
            pltpu.VMEM((GROUP, part, units), BF16),
            pltpu.VMEM((GROUP * units, part), BF16),
            pltpu.VMEM((batches, GROUP, rows, units), BF16),
            pltpu.VMEM((batches, GROUP, rows, units), BF16),
            pltpu.VMEM((rows, units), F32),
            pltpu.VMEM((batches, rows, GROUP * units), BF16),
            pltpu.VMEM((batches, rows, part), BF16),
            sem((GROUP,)),
            sem((GROUP,)),
            sem((GROUP,)),
            sem((GROUP,)),
            sem((3,)),
            sem((3,)),
            sem((batches, n)),
            sem((batches, n)),
            sem((batches, GROUP)),
            sem((batches, GROUP)),
            sem((batches, GROUP)),
            sem((batches, GROUP)),
            sem((batches, n)),
            sem((batches, n)),
            sem((2 + batches,)),
        ],
        compiler_params=pltpu.CompilerParams(
            collective_id=0, has_side_effects=True, vmem_limit_bytes=60 * 2**20
        ),
    )(
        place,
        activations[0],
        norm_gain,
        gate_values[0],
        up_weight[0].reshape(GROUP, part, units),
        down_weight[0],
    )

    finished = []
    for m in range(batches):
        expert_out = lax.dot_general(
            place_prev[m].reshape(experts * capacity, tok),
            returned[m],
            (((0,), (0,)), ((), ())),
            preferred_element_type=F32,
        )
        finished.append((act_prev[m].astype(F32) + gate_prev[m][:, None] * expert_out).astype(BF16))
    return jnp.stack(finished)[None]


SLOTS = 4
CHUNKS = 4


def quad_kernel(
    pipes, ids, act, gain, gate, up, down, out,
    ids_all, ids_prev, gate_prev, act_prev, place, dense, halves, x, mixed, wu, wd,
    pre, pre_send, pre_recv, hidden, results, ret, spread, gates, final,
    isend, irecv, ssend, srecv, nsend, nrecv, usend, urecv, dsend, drecv, osend, orecv, fsend, frecv,
    gsend, grecv, zsend, zrecv, msend, mrecv, psend, precv, hsend, hrecv, rsend, rrecv, own, wsem,
):
    me, pipe = lax.axis_index("expert"), lax.axis_index("pipe")
    z, y = me // 2, me % 2
    other = 1 - y
    half = z // 2
    s = (1 - half) * z + half * (3 - z)
    inner, outer = s == 1, s == 0
    batches, tok, width = act.shape
    wide = width // 2
    units = up.shape[1]
    capacity = x.shape[3]
    rows = 2 * SLOTS * capacity
    part = wide // CHUNKS
    ahead, behind = (pipe + 1) % pipes, (pipe + pipes - 1) % pipes

    def node(owner, slot, side):
        return ((1 - side) * slot + side * (3 - slot)) * 2 + owner

    beside, across, corner, mate = node(other, s, half), node(y, 1 - s, half), node(other, 1 - s, half), node(y, 1, 1 - half)

    barrier = pltpu.get_barrier_semaphore()

    def greet(**where):
        pl.semaphore_signal(barrier, inc=1, device_id=where, device_id_type=MESH)

    for device in (beside, across, corner):
        greet(expert=device)
    for owner in range(2):
        for side in range(2):
            greet(pipe=behind, expert=node(owner, 1, side))

    @pl.when(inner)
    def _():
        greet(expert=mate)
        pl.semaphore_wait(barrier, 4 + 8)

    @pl.when(outer)
    def _():
        greet(pipe=behind, expert=me)
        pl.semaphore_wait(barrier, 3 + 1)

    def wide_half(j):
        return pl.ds(pl.multiple_of(j * wide, 128), wide)

    def piece(c):
        return pl.ds(pl.multiple_of(c * part, 128), part)

    def piece_of(j, c):
        return pl.ds(pl.multiple_of(j * wide + c * part, 128), part)

    def share(j):
        return pl.ds(pl.multiple_of(j * units, 128), units)

    def id_copy(k, device, target):
        return remote(ids, target, isend.at[k], irecv.at[k], expert=device)

    id_out = [id_copy(k, device, ids_all.at[s, y]) for k, device in enumerate((beside, across, corner))]
    id_in = [
        id_copy(0, beside, ids_all.at[s, other]),
        id_copy(1, across, ids_all.at[1 - s, y]),
        id_copy(2, corner, ids_all.at[1 - s, other]),
    ]
    shifts = [
        remote(source, target, ssend.at[i], srecv.at[i], pipe=ahead)
        for i, (source, target) in enumerate(((ids, ids_prev), (gate, gate_prev), (act, act_prev)))
    ]

    def swap_rows(m, owner):
        return remote(halves.at[m], dense.at[m, s, owner], nsend.at[m], nrecv.at[m], expert=beside)

    def swap_up(j):
        return remote(up.at[wide_half(other), :], wu.at[:, share(j)], usend, urecv, expert=beside)

    def swap_down(c, j):
        return remote(
            down.at[:, piece_of(other, c)], wd.at[s, share(j), piece(c)], dsend.at[c], drecv.at[c], expert=beside
        )

    def lift_down(c):
        return remote(
            down.at[:, piece_of(y, c)], wd.at[0, share(y), piece(c)], osend.at[c], orecv.at[c], expert=across
        )

    def pass_down(c):
        block = wd.at[0, share(other), piece(c)]
        return remote(block, block, fsend.at[c], frecv.at[c], expert=across)

    def lift_rows(m, owner):
        block = dense.at[m, 0, owner]
        return remote(block, block, gsend.at[m, owner], grecv.at[m, owner], expert=across)

    def drop_rows(m, owner, slot):
        block = x.at[m, owner, slot]
        return remote(block, block, zsend.at[m, owner, slot], zrecv.at[m, owner, slot], expert=across)

    def cross(m, owner, slot):
        return remote(
            mixed.at[m, owner, slot], x.at[m, owner, 3 - slot], msend.at[m, owner, slot],
            mrecv.at[m, owner, slot], expert=mate,
        )

    def swap_pre(m):
        return remote(pre_send.at[m], pre_recv.at[m], psend.at[m], precv.at[m], expert=beside)

    def lift_hidden(m):
        block = hidden.at[m, 0]
        return remote(block, block, hsend.at[m], hrecv.at[m], expert=across)

    def give(m, c, owner, slot):
        index = owner * SLOTS + slot
        return remote(
            results.at[m, pl.ds(pl.multiple_of(index * capacity, 16), capacity), piece(c)],
            ret.at[m, y, pl.ds(pl.multiple_of(half * capacity, 16), capacity), piece(c)],
            rsend.at[m, c, index], rrecv.at[m, c, half, y], pipe=ahead, expert=node(owner, slot, half),
        )

    def taken(m, c, expert, j):
        return remote(
            results.at[m, pl.ds(0, capacity), piece(c)],
            ret.at[m, j, pl.ds(pl.multiple_of(expert * capacity, 16), capacity), piece(c)],
            rsend.at[m, c, 0], rrecv.at[m, c, expert, j], pipe=ahead,
        )

    def written(m, c, j):
        columns = piece_of(j, c)
        return pltpu.make_async_copy(final.at[m, :, columns], out.at[m, :, columns], wsem.at[m, c, j])

    own_up = pltpu.make_async_copy(up.at[wide_half(y), :], wu.at[:, share(y)], own.at[0])
    own_down = pltpu.make_async_copy(down.at[:, wide_half(y)], wd.at[1, share(y), :], own.at[1])

    for copy in id_out:
        copy.start()
    own_up.start()

    def normalise(m):
        mine = act[m, :, wide_half(y)].astype(F32)
        far = act[m, :, wide_half(other)].astype(F32)
        total = jnp.sum(mine * mine, axis=-1, keepdims=True) + jnp.sum(far * far, axis=-1, keepdims=True)
        scale = lax.rsqrt(total / width + EPSILON)
        halves[m] = (far * scale * gain[:, wide_half(other)].astype(F32)).astype(BF16)
        swap_rows(m, y).start()
        dense[m, s, y] = (mine * scale * gain[:, wide_half(y)].astype(F32)).astype(BF16)

    normalise(0)

    @pl.when(outer)
    def _():
        lift_rows(0, y).start()

    normalise(1)
    ids_all[s, y] = ids[...]
    for copy in id_in:
        copy.wait_recv()

    lane = lax.broadcasted_iota(jnp.int32, (tok, tok), 1)
    line = lax.broadcasted_iota(jnp.int32, (tok, tok), 0)
    earlier = (line < lane).astype(BF16)
    slot_line = lax.broadcasted_iota(jnp.int32, (capacity, tok), 0).astype(F32)
    expert_line = lax.broadcasted_iota(jnp.int32, (16, tok), 0)
    for slot in range(2):
        for owner in range(2):
            for m in range(batches):
                onehot = (ids_all[slot, owner, m : m + 1, :] == expert_line).astype(F32)
                before = jnp.dot(onehot.astype(BF16), earlier, preferred_element_type=F32)
                for e in range(2):
                    hit = jnp.where(before[e : e + 1] == slot_line, onehot[e : e + 1], 0.0)
                    place[slot, owner, m, e] = hit.astype(BF16)

    def pack(m, slot, owner, expert):
        return jnp.dot(
            place[slot, owner, m, expert], dense[m, slot, owner], preferred_element_type=F32
        ).astype(BF16)

    def keep(m, slot, owner):
        x[m, owner, slot] = pack(m, slot, owner, half)

    def pack_cross(m, slot, owner):
        mixed[m, owner, slot] = pack(m, slot, owner, 1 - half)
        cross(m, owner, slot).start()

    def pack_inner(m, owner):
        keep(m, 1, owner)
        drop_rows(m, owner, 1).start()
        pack_cross(m, 1, owner)

    def lifted(m, owner):
        lift_rows(m, owner).wait_recv()
        pack_cross(m, 0, owner)
        keep(m, 0, owner)

    def forward(m, owner, slot):
        cross(m, owner, 3 - slot).wait_recv()
        drop_rows(m, owner, slot).start()

    def partial(m):
        total = jnp.dot(x[m].reshape(rows, wide), wu[...], preferred_element_type=F32)
        pre_send[m] = total.astype(BF16)
        swap_pre(m).start()
        pre[m] = total

    def activate(m):
        swap_pre(m).wait_recv()
        hidden[m, s] = jax.nn.silu(pre[m] + pre_recv[m].astype(F32)).astype(BF16)

    @pl.when(inner)
    def _():
        own_down.start()
        pack_inner(0, y)
        swap_rows(0, other).wait_recv()
        swap_up(y).start()
        pack_inner(0, other)
        pack_inner(1, y)
        forward(0, y, 2)
        lifted(0, y)
        swap_rows(1, other).wait_recv()
        pack_inner(1, other)
        forward(0, other, 2)
        lifted(0, other)
        forward(0, y, 3)
        forward(1, y, 2)
        lifted(1, y)
        forward(0, other, 3)
        forward(1, other, 2)
        lifted(1, other)
        for copy in shifts:
            copy.start()
        forward(1, y, 3)
        forward(1, other, 3)
        own_up.wait()
        swap_up(other).wait_recv()
        partial(0)
        each(0, CHUNKS, lambda c: swap_down(c, y).start())
        partial(1)
        activate(0)
        activate(1)
        own_down.wait()

    @pl.when(outer)
    def _():
        keep(0, 0, y)
        keep(1, 0, y)
        swap_rows(0, other).wait_recv()
        swap_up(y).start()
        lift_rows(0, other).start()
        lift_rows(1, y).start()
        keep(0, 0, other)
        swap_rows(1, other).wait_recv()
        lift_rows(1, other).start()
        keep(1, 0, other)
        for copy in shifts:
            copy.start()
        for m in range(batches):
            for owner in range(2):
                lift_rows(m, owner).wait_send()
        each(0, CHUNKS, lambda c: lift_down(c).start())
        own_up.wait()
        swap_up(other).wait_recv()

        def gathered(m):
            for slot in range(1, SLOTS):
                for owner in range(2):
                    drop_rows(m, owner, slot).wait_recv()

        def relay(c):
            swap_down(c, other).wait_recv()
            pass_down(c).start()

        gathered(0)
        partial(0)
        each(0, CHUNKS, lambda c: swap_down(c, y).start())
        activate(0)
        lift_hidden(0).start()
        relay(0)
        relay(1)
        gathered(1)
        partial(1)
        relay(2)
        activate(1)
        lift_hidden(1).start()
        relay(3)

    for copy in shifts:
        copy.wait_recv()
    later = (lane < line).astype(BF16)
    same = lane == line
    expert_lane = lax.broadcasted_iota(jnp.int32, (tok, 128), 1).astype(F32)
    slot_lane = lax.broadcasted_iota(jnp.int32, (tok, 2 * capacity), 1).astype(F32)
    for m in range(batches):
        chosen = jnp.sum(jnp.where(same, ids_prev[m : m + 1, :].astype(F32), 0.0), axis=1, keepdims=True)
        onehot = (chosen == expert_lane).astype(F32)
        before = jnp.dot(later, onehot.astype(BF16), preferred_element_type=F32)
        slot = chosen * capacity + jnp.sum(before * onehot, axis=1, keepdims=True)
        spread[m] = (slot == slot_lane).astype(BF16)
        gates[m] = jnp.sum(jnp.where(same, gate_prev[m : m + 1, :], 0.0), axis=1, keepdims=True)

    def produce(step):
        m, c = step // CHUNKS, step % CHUNKS

        @pl.when(c == 0)
        def _():
            lift_hidden(m).wait_recv()

        @pl.when(m == 0)
        def _():
            lift_down(c).wait_recv()
            swap_down(c, other).wait_recv()
            pass_down(c).wait_recv()

        total = jnp.dot(hidden[m, 0], wd[0, :, piece(c)], preferred_element_type=F32)
        total = total + jnp.dot(hidden[m, 1], wd[1, :, piece(c)], preferred_element_type=F32)
        results[m, :, piece(c)] = total.astype(BF16)
        for slot in (3, 2, 0, 1):
            for owner in range(2):
                give(m, c, owner, slot).start()

    def finish(step):
        m, c = step // CHUNKS, step % CHUNKS
        for j in range(2):
            for expert in range(2):
                taken(m, c, expert, j).wait_recv()
            columns = piece_of(j, c)
            expert_out = jnp.dot(spread[m], ret[m, j, :, piece(c)], preferred_element_type=F32)
            final[m, :, columns] = (act_prev[m, :, columns].astype(F32) + gates[m] * expert_out).astype(BF16)
            written(m, c, j).start()

    steps = batches * CHUNKS

    @pl.when(inner)
    def _():
        each(0, 2, produce)

        def both(step):
            produce(step)
            finish(step - 2)

        each(2, steps, both)
        each(steps - 2, steps, finish)

    @pl.when(outer)
    def _():
        each(0, steps, finish)

    for copy in id_out + shifts:
        copy.wait_send()
    swap_up(y).wait_send()
    each(0, CHUNKS, lambda c: swap_down(c, y).wait_send())
    for m in range(batches):
        swap_rows(m, y).wait_send()
        swap_pre(m).wait_send()

    @pl.when(inner)
    def _():
        for m in range(batches):
            for owner in range(2):
                for slot in range(1, SLOTS):
                    drop_rows(m, owner, slot).wait_send()
                for slot in range(2):
                    cross(m, owner, slot).wait_send()

        def sent(step):
            m, c = step // CHUNKS, step % CHUNKS
            for slot in range(SLOTS):
                for owner in range(2):
                    give(m, c, owner, slot).wait_send()

        each(0, steps, sent)

    @pl.when(outer)
    def _():
        for m in range(batches):
            lift_hidden(m).wait_send()

        def sent(c):
            lift_down(c).wait_send()
            pass_down(c).wait_send()

        each(0, CHUNKS, sent)

    def stored(step):
        for j in range(2):
            written(step // CHUNKS, step % CHUNKS, j).wait()

    each(0, steps, stored)


def paired(pipes, activations, expert_ids, gate_values, norm_gain, up_weight, down_weight):
    _, batches, tok, width = activations.shape
    wide = width // 2
    units = up_weight.shape[2]
    capacity = (3 * tok // 4 + 15) // 16 * 16
    rows = 2 * SLOTS * capacity
    vmem, far = pl.BlockSpec(memory_space=pltpu.VMEM), pl.BlockSpec(memory_space=pl.ANY)
    room, sem = pltpu.VMEM, pltpu.SemaphoreType.DMA
    received = pl.pallas_call(
        functools.partial(quad_kernel, pipes),
        out_shape=jax.ShapeDtypeStruct((batches, tok, width), BF16),
        in_specs=[vmem] * 4 + [far] * 2,
        out_specs=far,
        scratch_shapes=[
            room((2, 2, batches, tok), jnp.int32),
            room((batches, tok), jnp.int32),
            room((batches, tok), F32),
            room((batches, tok, width), BF16),
            room((2, 2, batches, 2, capacity, tok), BF16),
            room((batches, 2, 2, tok, wide), BF16),
            room((batches, tok, wide), BF16),
            room((batches, 2, SLOTS, capacity, wide), BF16),
            room((batches, 2, 2, capacity, wide), BF16),
            room((wide, 2 * units), BF16),
            room((2, 2 * units, wide), BF16),
            room((batches, rows, 2 * units), F32),
            room((batches, rows, 2 * units), BF16),
            room((batches, rows, 2 * units), BF16),
            room((batches, 2, rows, 2 * units), BF16),
            room((batches, rows, wide), BF16),
            room((batches, 2, 2 * capacity, wide), BF16),
            room((batches, tok, 2 * capacity), BF16),
            room((batches, tok, 1), F32),
            room((batches, tok, width), BF16),
            sem((3,)), sem((3,)),
            sem((3,)), sem((3,)),
            sem((batches,)), sem((batches,)),
            sem, sem,
            sem((CHUNKS,)), sem((CHUNKS,)),
            sem((CHUNKS,)), sem((CHUNKS,)),
            sem((CHUNKS,)), sem((CHUNKS,)),
            sem((batches, 2)), sem((batches, 2)),
            sem((batches, 2, SLOTS)), sem((batches, 2, SLOTS)),
            sem((batches, 2, 2)), sem((batches, 2, 2)),
            sem((batches,)), sem((batches,)),
            sem((batches,)), sem((batches,)),
            sem((batches, CHUNKS, 2 * SLOTS)), sem((batches, CHUNKS, 2, 2)),
            sem((2,)),
            sem((batches, CHUNKS, 2)),
        ],
        compiler_params=pltpu.CompilerParams(
            collective_id=1, has_side_effects=True, vmem_limit_bytes=60 * 2**20
        ),
    )(expert_ids[0], activations[0], norm_gain, gate_values[0], up_weight[0], down_weight[0])
    return received[None]


def local(pipes, *arrays):
    if lax.axis_size("expert") == 2 * GROUP:
        return paired(pipes, *arrays)
    return general(pipes, *arrays)


def solution(mesh):
    placed = (
        P("pipe", None, "expert", None),
        P("pipe", None, "expert"),
        P("pipe", None, "expert"),
        P("pipe", None),
        P("pipe", None, "expert"),
        P("pipe", "expert", None),
    )
    return jax.shard_map(
        functools.partial(local, mesh.shape["pipe"]),
        mesh=mesh,
        in_specs=placed,
        out_specs=P("pipe", None, "expert", None),
        check_vma=False,
    )
```

```python
import functools

import jax
import jax.numpy as jnp
from jax import lax
from jax.experimental import pallas as pl
from jax.experimental.pallas import tpu as pltpu
from jax.sharding import PartitionSpec as P

LEVELS = 2


EPSILON = 1e-06
GROUP = 2**LEVELS
MESH = pl.DeviceIdType.MESH
F32, BF16 = jnp.float32, jnp.bfloat16


def remote(source, target, send, recv, **where):
    return pltpu.make_async_remote_copy(
        src_ref=source, dst_ref=target, send_sem=send, recv_sem=recv, device_id=where, device_id_type=MESH
    )


def each(low, high, body):
    def step(index, carry):
        body(index)
        return carry

    lax.fori_loop(low, high, step, 0)


def layer_kernel(
    n, pipes, place, act, gain, gate, up, down, ret, act_out, place_out, gate_out,
    packed, x, up_all, down_all, pres, sums, own_pre, hidden, out,
    usend, urecv, dsend, drecv, psend, precv, xsend, xrecv, ssend, srecv, hsend, hrecv, rsend, rrecv, own,
):
    me, pipe = lax.axis_index("expert"), lax.axis_index("pipe")
    group_index = me // GROUP
    first = group_index * GROUP
    g = me - first
    batches, experts, capacity = place.shape[:3]
    part, units = up.shape[1:]
    ahead, behind = (pipe + 1) % pipes, (pipe + pipes - 1) % pipes
    blocks = n // GROUP
    tall = GROUP * capacity

    barrier = pltpu.get_barrier_semaphore()

    def greet(k):
        pl.semaphore_signal(barrier, inc=1, device_id={"expert": (me + k) % n}, device_id_type=MESH)

    def greet_behind(k):
        pl.semaphore_signal(barrier, inc=1, device_id={"pipe": behind, "expert": k}, device_id_type=MESH)

    each(1, n, greet)
    each(0, n, greet_behind)
    pl.semaphore_wait(barrier, 2 * n - 1)

    def columns(j):
        return pl.ds(pl.multiple_of(j * part, 128), part)

    def share(j):
        return pl.ds(pl.multiple_of(j * units, 128), units)

    def rows_of(d):
        return pl.ds(pl.multiple_of(d * capacity, 16), capacity)

    peers = [(k, (g + k) % GROUP) for k in range(1, GROUP)]
    ups = [remote(up.at[j], up_all.at[g], usend.at[k], urecv.at[k], expert=first + j) for k, j in peers]
    downs = [
        remote(
            down.at[:, columns(j)], down_all.at[share(g), :], dsend.at[k], drecv.at[k], expert=first + j
        )
        for k, j in peers
    ]
    shifts = [
        remote(source, target, psend.at[i], precv.at[i], pipe=ahead)
        for i, (source, target) in enumerate(((act, act_out), (place, place_out), (gate, gate_out)))
    ]

    def dispatch(m, k):
        d = (me + k) % n
        return remote(packed.at[m, d], x.at[m, rows_of(me), :], xsend.at[m, k], xrecv.at[m, k], expert=d)

    for copy in ups:
        copy.start()
    own_up = pltpu.make_async_copy(up.at[g], up_all.at[g], own.at[0])
    own_down = pltpu.make_async_copy(down.at[:, columns(g)], down_all.at[share(g), :], own.at[1])
    own_up.start()
    own_down.start()
    own_rows = []
    for m in range(batches):
        wide = act[m].astype(F32)
        scale = lax.rsqrt(jnp.mean(wide * wide, axis=-1, keepdims=True) + EPSILON)
        normed = (wide * scale * gain[...].astype(F32)).astype(BF16)
        for e in range(experts):
            for j in range(GROUP):
                packed[m, e * GROUP + j] = jnp.dot(
                    place[m, e], normed[:, j * part : (j + 1) * part], preferred_element_type=F32
                ).astype(BF16)
        if m == 0:
            each(1, n, lambda k: dispatch(0, k).start())
        copy = pltpu.make_async_copy(packed.at[m, me], x.at[m, rows_of(me), :], own.at[2 + m])
        copy.start()
        own_rows.append(copy)

    def summing(m, k, j):
        return remote(pres.at[m, k], sums.at[m, k], ssend.at[m, k], srecv.at[m, k], expert=first + j)

    def sharing(m, k, j):
        mine = hidden.at[m, :, share(g)]
        return remote(mine, mine, hsend.at[m, k], hrecv.at[m, k], expert=first + j)

    own_up.wait()
    for copy in ups:
        copy.wait_recv()
    for m in range(batches):
        own_rows[m].wait()
        each(1, n, lambda k, m=m: dispatch(m, k).wait_recv())
        for k, j in peers:
            pres[m, k] = jnp.dot(x[m], up_all[j], preferred_element_type=F32).astype(BF16)
            summing(m, k, j).start()
        if m + 1 < batches:
            each(1, n, lambda k, m=m: dispatch(m + 1, k).start())
        if m == 0:
            for copy in downs + shifts:
                copy.start()
        own_pre[...] = jnp.dot(x[m], up_all[g], preferred_element_type=F32)
        for k, j in peers:
            summing(m, k, j).wait_recv()
        total = own_pre[...]
        for k in range(1, GROUP):
            total = total + sums[m, k].astype(F32)
        hidden[m, :, share(g)] = jax.nn.silu(total).astype(BF16)
        for k, j in peers:
            sharing(m, k, j).start()

    def slots_of(m, source):
        return ret.at[m, rows_of(source // GROUP), columns(source % GROUP)]

    def give(m, target):
        return remote(
            out.at[m, rows_of(target), :], slots_of(m, me), rsend.at[m, target], rrecv.at[m, me],
            pipe=ahead, expert=target,
        )

    own_down.wait()
    for copy in downs:
        copy.wait_recv()
    for m in range(batches):
        for k, j in peers:
            sharing(m, k, j).wait_recv()

        def block(index, m=m):
            owner = (group_index + 1 + index) % blocks
            rows = pl.ds(pl.multiple_of(owner * tall, 16), tall)
            out[m, rows, :] = jnp.dot(
                hidden[m, rows, :], down_all[...], preferred_element_type=F32
            ).astype(BF16)
            for j in range(GROUP):
                give(m, owner * GROUP + j).start()

        each(0, blocks, block)

    for copy in ups + downs:
        copy.wait_send()
    for copy in shifts:
        copy.wait()
    for m in range(batches):
        each(1, n, lambda k, m=m: dispatch(m, k).wait_send())
        for k, j in peers:
            summing(m, k, j).wait_send()
            sharing(m, k, j).wait_send()

        def finish(source, m=m):
            give(m, source).wait_send()
            remote(
                out.at[m, rows_of(source), :], slots_of(m, source), rsend.at[m, source],
                rrecv.at[m, source], pipe=ahead, expert=source,
            ).wait_recv()

        each(0, n, finish)


def general(pipes, activations, expert_ids, gate_values, norm_gain, up_weight, down_weight):
    n = lax.axis_size("expert")
    experts = n // GROUP
    _, batches, tok, width = activations.shape
    part = width // GROUP
    units = up_weight.shape[2]
    capacity = max(2, 3 * tok // (2 * experts))
    capacity = (capacity + 15) // 16 * 16
    rows = n * capacity

    order = jnp.arange(tok, dtype=jnp.int32)
    same = expert_ids[0][:, :, None] == expert_ids[0][:, None, :]
    ranking = jnp.sum((same & (order[None, :] < order[:, None])).astype(jnp.int32), axis=-1)
    slot = expert_ids[0] * capacity + ranking
    slots = jnp.arange(experts * capacity, dtype=jnp.int32).reshape(1, experts, capacity, 1)
    place = (slot[:, None, None, :] == slots).astype(BF16)

    vmem, far = pl.BlockSpec(memory_space=pltpu.VMEM), pl.BlockSpec(memory_space=pl.ANY)
    shape, sem = jax.ShapeDtypeStruct, pltpu.SemaphoreType.DMA
    returned, act_prev, place_prev, gate_prev = pl.pallas_call(
        functools.partial(layer_kernel, n, pipes),
        out_shape=(
            shape((batches, experts * capacity, width), BF16),
            shape((batches, tok, width), BF16),
            shape(place.shape, BF16),
            shape((batches, tok), F32),
        ),
        in_specs=[vmem] * 4 + [far] * 2,
        out_specs=(far,) * 4,
        scratch_shapes=[
            pltpu.VMEM((batches, n, capacity, part), BF16),
            pltpu.VMEM((batches, rows, part), BF16),
            pltpu.VMEM((GROUP, part, units), BF16),
            pltpu.VMEM((GROUP * units, part), BF16),
            pltpu.VMEM((batches, GROUP, rows, units), BF16),
            pltpu.VMEM((batches, GROUP, rows, units), BF16),
            pltpu.VMEM((rows, units), F32),
            pltpu.VMEM((batches, rows, GROUP * units), BF16),
            pltpu.VMEM((batches, rows, part), BF16),
            sem((GROUP,)),
            sem((GROUP,)),
            sem((GROUP,)),
            sem((GROUP,)),
            sem((3,)),
            sem((3,)),
            sem((batches, n)),
            sem((batches, n)),
            sem((batches, GROUP)),
            sem((batches, GROUP)),
            sem((batches, GROUP)),
            sem((batches, GROUP)),
            sem((batches, n)),
            sem((batches, n)),
            sem((2 + batches,)),
        ],
        compiler_params=pltpu.CompilerParams(
            collective_id=0, has_side_effects=True, vmem_limit_bytes=60 * 2**20
        ),
    )(
        place,
        activations[0],
        norm_gain,
        gate_values[0],
        up_weight[0].reshape(GROUP, part, units),
        down_weight[0],
    )

    finished = []
    for m in range(batches):
        expert_out = lax.dot_general(
            place_prev[m].reshape(experts * capacity, tok),
            returned[m],
            (((0,), (0,)), ((), ())),
            preferred_element_type=F32,
        )
        finished.append((act_prev[m].astype(F32) + gate_prev[m][:, None] * expert_out).astype(BF16))
    return jnp.stack(finished)[None]


SLOTS = 4
CHUNKS = 4
LAG = 4


def quad_kernel(
    pipes, ids, act, gain, gate, up, down, out,
    ids_all, ids_prev, gate_prev, act_prev, place, dense, halves, x, mixed, wu, wd,
    pre, pre_send, pre_recv, hidden, results, ret, spread, gates, final,
    isend, irecv, ssend, srecv, nsend, nrecv, usend, urecv, dsend, drecv, osend, orecv, fsend, frecv,
    gsend, grecv, zsend, zrecv, msend, mrecv, psend, precv, hsend, hrecv, rsend, rrecv, own, wsem,
):
    me, pipe = lax.axis_index("expert"), lax.axis_index("pipe")
    z, y = me // 2, me % 2
    other = 1 - y
    half = z // 2
    s = (1 - half) * z + half * (3 - z)
    inner, outer = s == 1, s == 0
    batches, tok, width = act.shape
    wide = width // 2
    units = up.shape[1]
    capacity = x.shape[3]
    rows = 2 * SLOTS * capacity
    part = wide // CHUNKS
    ahead, behind = (pipe + 1) % pipes, (pipe + pipes - 1) % pipes

    def node(owner, slot, side):
        return ((1 - side) * slot + side * (3 - slot)) * 2 + owner

    beside, across, corner, mate = node(other, s, half), node(y, 1 - s, half), node(other, 1 - s, half), node(y, 1, 1 - half)

    barrier = pltpu.get_barrier_semaphore()

    def greet(**where):
        pl.semaphore_signal(barrier, inc=1, device_id=where, device_id_type=MESH)

    for device in (beside, across, corner):
        greet(expert=device)
    for owner in range(2):
        for side in range(2):
            greet(pipe=behind, expert=node(owner, 1, side))

    @pl.when(inner)
    def _():
        greet(expert=mate)
        pl.semaphore_wait(barrier, 4 + 8)

    @pl.when(outer)
    def _():
        greet(pipe=behind, expert=me)
        pl.semaphore_wait(barrier, 3 + 1)

    def wide_half(j):
        return pl.ds(pl.multiple_of(j * wide, 128), wide)

    def piece(c):
        return pl.ds(pl.multiple_of(c * part, 128), part)

    def piece_of(j, c):
        return pl.ds(pl.multiple_of(j * wide + c * part, 128), part)

    def share(j):
        return pl.ds(pl.multiple_of(j * units, 128), units)

    def id_copy(k, device, target):
        return remote(ids, target, isend.at[k], irecv.at[k], expert=device)

    id_out = [id_copy(k, device, ids_all.at[s, y]) for k, device in enumerate((beside, across, corner))]
    id_in = [
        id_copy(0, beside, ids_all.at[s, other]),
        id_copy(1, across, ids_all.at[1 - s, y]),
        id_copy(2, corner, ids_all.at[1 - s, other]),
    ]
    shifts = [
        remote(source, target, ssend.at[i], srecv.at[i], pipe=ahead)
        for i, (source, target) in enumerate(((ids, ids_prev), (gate, gate_prev), (act, act_prev)))
    ]

    def swap_rows(m, owner):
        return remote(halves.at[m], dense.at[m, s, owner], nsend.at[m], nrecv.at[m], expert=beside)

    def swap_up(j):
        return remote(up.at[wide_half(other), :], wu.at[:, share(j)], usend, urecv, expert=beside)

    def swap_down(c, j):
        return remote(
            down.at[:, piece_of(other, c)], wd.at[s, share(j), piece(c)], dsend.at[c], drecv.at[c], expert=beside
        )

    def lift_down(c):
        return remote(
            down.at[:, piece_of(y, c)], wd.at[0, share(y), piece(c)], osend.at[c], orecv.at[c], expert=across
        )

    def pass_down(c):
        block = wd.at[0, share(other), piece(c)]
        return remote(block, block, fsend.at[c], frecv.at[c], expert=across)

    def lift_rows(m, owner):
        block = dense.at[m, 0, owner]
        return remote(block, block, gsend.at[m, owner], grecv.at[m, owner], expert=across)

    def drop_rows(m, owner, slot):
        block = x.at[m, owner, slot]
        return remote(block, block, zsend.at[m, owner, slot], zrecv.at[m, owner, slot], expert=across)

    def cross(m, owner, slot):
        return remote(
            mixed.at[m, owner, slot], x.at[m, owner, 3 - slot], msend.at[m, owner, slot],
            mrecv.at[m, owner, slot], expert=mate,
        )

    def swap_pre(m):
        return remote(pre_send.at[m], pre_recv.at[m], psend.at[m], precv.at[m], expert=beside)

    def lift_hidden(m):
        block = hidden.at[m, 0]
        return remote(block, block, hsend.at[m], hrecv.at[m], expert=across)

    def give(m, c, owner, slot):
        index = owner * SLOTS + slot
        return remote(
            results.at[m, pl.ds(pl.multiple_of(index * capacity, 16), capacity), piece(c)],
            ret.at[m, y, pl.ds(pl.multiple_of(half * capacity, 16), capacity), piece(c)],
            rsend.at[m, c, index], rrecv.at[m, c, half, y], pipe=ahead, expert=node(owner, slot, half),
        )

    def taken(m, c, expert, j):
        return remote(
            results.at[m, pl.ds(0, capacity), piece(c)],
            ret.at[m, j, pl.ds(pl.multiple_of(expert * capacity, 16), capacity), piece(c)],
            rsend.at[m, c, 0], rrecv.at[m, c, expert, j], pipe=ahead,
        )

    def written(m, c, j):
        columns = piece_of(j, c)
        return pltpu.make_async_copy(final.at[m, :, columns], out.at[m, :, columns], wsem.at[m, c, j])

    own_up = pltpu.make_async_copy(up.at[wide_half(y), :], wu.at[:, share(y)], own.at[0])
    own_down = pltpu.make_async_copy(down.at[:, wide_half(y)], wd.at[1, share(y), :], own.at[1])

    for copy in id_out:
        copy.start()
    own_up.start()

    def normalise(m):
        mine = act[m, :, wide_half(y)].astype(F32)
        far = act[m, :, wide_half(other)].astype(F32)
        total = jnp.sum(mine * mine, axis=-1, keepdims=True) + jnp.sum(far * far, axis=-1, keepdims=True)
        scale = lax.rsqrt(total / width + EPSILON)
        halves[m] = (far * scale * gain[:, wide_half(other)].astype(F32)).astype(BF16)
        swap_rows(m, y).start()
        dense[m, s, y] = (mine * scale * gain[:, wide_half(y)].astype(F32)).astype(BF16)

    normalise(0)

    @pl.when(outer)
    def _():
        lift_rows(0, y).start()

    normalise(1)
    ids_all[s, y] = ids[...]
    for copy in id_in:
        copy.wait_recv()

    lane = lax.broadcasted_iota(jnp.int32, (tok, tok), 1)
    line = lax.broadcasted_iota(jnp.int32, (tok, tok), 0)
    earlier = (line < lane).astype(BF16)
    slot_line = lax.broadcasted_iota(jnp.int32, (capacity, tok), 0).astype(F32)
    expert_line = lax.broadcasted_iota(jnp.int32, (16, tok), 0)
    for slot in range(2):
        for owner in range(2):
            for m in range(batches):
                onehot = (ids_all[slot, owner, m : m + 1, :] == expert_line).astype(F32)
                before = jnp.dot(onehot.astype(BF16), earlier, preferred_element_type=F32)
                for e in range(2):
                    hit = jnp.where(before[e : e + 1] == slot_line, onehot[e : e + 1], 0.0)
                    place[slot, owner, m, e] = hit.astype(BF16)

    def pack(m, slot, owner, expert):
        return jnp.dot(
            place[slot, owner, m, expert], dense[m, slot, owner], preferred_element_type=F32
        ).astype(BF16)

    def keep(m, slot, owner):
        x[m, owner, slot] = pack(m, slot, owner, half)

    def pack_cross(m, slot, owner):
        mixed[m, owner, slot] = pack(m, slot, owner, 1 - half)
        cross(m, owner, slot).start()

    def pack_inner(m, owner):
        keep(m, 1, owner)
        drop_rows(m, owner, 1).start()
        pack_cross(m, 1, owner)

    def lifted(m, owner):
        lift_rows(m, owner).wait_recv()
        pack_cross(m, 0, owner)
        keep(m, 0, owner)

    def forward(m, owner, slot):
        cross(m, owner, 3 - slot).wait_recv()
        drop_rows(m, owner, slot).start()

    def partial(m):
        total = jnp.dot(x[m].reshape(rows, wide), wu[...], preferred_element_type=F32)
        pre_send[m] = total.astype(BF16)
        swap_pre(m).start()
        pre[m] = total

    def activate(m):
        swap_pre(m).wait_recv()
        hidden[m, s] = jax.nn.silu(pre[m] + pre_recv[m].astype(F32)).astype(BF16)

    @pl.when(inner)
    def _():
        own_down.start()
        pack_inner(0, y)
        swap_rows(0, other).wait_recv()
        swap_up(y).start()
        swap_down(0, y).start()
        pack_inner(0, other)
        lifted(0, y)
        forward(0, y, 2)
        forward(0, other, 2)
        lifted(0, other)
        pack_cross(1, 1, y)
        swap_rows(1, other).wait_recv()
        pack_cross(1, 1, other)
        forward(0, y, 3)
        lifted(1, y)
        forward(0, other, 3)
        for owner in (y, other):
            keep(1, 1, owner)
            drop_rows(1, owner, 1).start()
        lifted(1, other)
        forward(1, y, 2)
        forward(1, other, 2)
        for copy in shifts:
            copy.start()
        own_up.wait()
        swap_up(other).wait_recv()
        partial(0)
        each(1, CHUNKS - 1, lambda c: swap_down(c, y).start())
        forward(1, y, 3)
        forward(1, other, 3)
        partial(1)
        swap_down(CHUNKS - 1, y).start()
        own_down.wait()

    @pl.when(outer)
    def _():
        keep(0, 0, y)
        keep(1, 0, y)
        swap_rows(0, other).wait_recv()
        swap_up(y).start()
        swap_down(0, y).start()
        lift_rows(0, other).start()
        lift_rows(1, y).start()
        keep(0, 0, other)
        swap_rows(1, other).wait_recv()
        lift_rows(1, other).start()
        each(0, CHUNKS - 1, lambda c: lift_down(c).start())
        keep(1, 0, other)
        for copy in shifts:
            copy.start()
        own_up.wait()

        def gathered(m):
            for slot in range(1, SLOTS):
                for owner in range(2):
                    drop_rows(m, owner, slot).wait_recv()

        def relay(c):
            swap_down(c, other).wait_recv()
            pass_down(c).start()

        gathered(0)
        swap_up(other).wait_recv()
        partial(0)
        each(1, CHUNKS - 1, lambda c: swap_down(c, y).start())
        relay(0)
        activate(0)
        lift_hidden(0).start()
        each(1, CHUNKS - 2, relay)
        gathered(1)
        partial(1)
        swap_down(CHUNKS - 1, y).start()
        relay(CHUNKS - 2)
        activate(1)
        lift_hidden(1).start()
        lift_down(CHUNKS - 1).start()
        relay(CHUNKS - 1)

    for copy in shifts:
        copy.wait_recv()
    later = (lane < line).astype(BF16)
    same = lane == line
    expert_lane = lax.broadcasted_iota(jnp.int32, (tok, 128), 1).astype(F32)
    slot_lane = lax.broadcasted_iota(jnp.int32, (tok, 2 * capacity), 1).astype(F32)
    for m in range(batches):
        chosen = jnp.sum(jnp.where(same, ids_prev[m : m + 1, :].astype(F32), 0.0), axis=1, keepdims=True)
        onehot = (chosen == expert_lane).astype(F32)
        before = jnp.dot(later, onehot.astype(BF16), preferred_element_type=F32)
        slot = chosen * capacity + jnp.sum(before * onehot, axis=1, keepdims=True)
        spread[m] = (slot == slot_lane).astype(BF16)
        gates[m] = jnp.sum(jnp.where(same, gate_prev[m : m + 1, :], 0.0), axis=1, keepdims=True)

    def place_of(step):
        first = CHUNKS - 1
        late = step // (2 * first)
        return (1 - late) * (step // first) + late * (step - 2 * first), (1 - late) * (step % first) + late * first

    def produce(step):
        m, c = place_of(step)

        @pl.when(c == 0)
        def _():
            activate(m)
            lift_hidden(m).wait_recv()

        @pl.when(m == 0)
        def _():
            lift_down(c).wait_recv()
            swap_down(c, other).wait_recv()
            pass_down(c).wait_recv()

        total = jnp.dot(hidden[m, 0], wd[0, :, piece(c)], preferred_element_type=F32)
        total = total + jnp.dot(hidden[m, 1], wd[1, :, piece(c)], preferred_element_type=F32)
        results[m, :, piece(c)] = total.astype(BF16)
        for slot in (3, 2, 0, 1):
            for owner in range(2):
                give(m, c, owner, slot).start()

    def finish(step):
        m, c = place_of(step)
        for j in range(2):
            for expert in range(2):
                taken(m, c, expert, j).wait_recv()
            columns = piece_of(j, c)
            expert_out = jnp.dot(spread[m], ret[m, j, :, piece(c)], preferred_element_type=F32)
            final[m, :, columns] = (act_prev[m, :, columns].astype(F32) + gates[m] * expert_out).astype(BF16)
            written(m, c, j).start()

    steps = batches * CHUNKS

    @pl.when(inner)
    def _():
        each(0, LAG, produce)

        def both(step):
            produce(step)
            finish(step - LAG)

        each(LAG, steps, both)
        each(steps - LAG, steps, finish)

    @pl.when(outer)
    def _():
        each(0, steps, finish)

    for copy in id_out + shifts:
        copy.wait_send()
    swap_up(y).wait_send()
    each(0, CHUNKS, lambda c: swap_down(c, y).wait_send())
    for m in range(batches):
        swap_rows(m, y).wait_send()
        swap_pre(m).wait_send()

    @pl.when(inner)
    def _():
        for m in range(batches):
            for owner in range(2):
                for slot in range(1, SLOTS):
                    drop_rows(m, owner, slot).wait_send()
                for slot in range(2):
                    cross(m, owner, slot).wait_send()

        def sent(step):
            m, c = step // CHUNKS, step % CHUNKS
            for slot in range(SLOTS):
                for owner in range(2):
                    give(m, c, owner, slot).wait_send()

        each(0, steps, sent)

    @pl.when(outer)
    def _():
        for m in range(batches):
            lift_hidden(m).wait_send()
            for owner in range(2):
                lift_rows(m, owner).wait_send()

        def sent(c):
            lift_down(c).wait_send()
            pass_down(c).wait_send()

        each(0, CHUNKS, sent)

    def stored(step):
        for j in range(2):
            written(step // CHUNKS, step % CHUNKS, j).wait()

    each(0, steps, stored)


def paired(pipes, activations, expert_ids, gate_values, norm_gain, up_weight, down_weight):
    _, batches, tok, width = activations.shape
    wide = width // 2
    units = up_weight.shape[2]
    capacity = (3 * tok // 4 + 15) // 16 * 16
    rows = 2 * SLOTS * capacity
    vmem, far = pl.BlockSpec(memory_space=pltpu.VMEM), pl.BlockSpec(memory_space=pl.ANY)
    room, sem = pltpu.VMEM, pltpu.SemaphoreType.DMA
    received = pl.pallas_call(
        functools.partial(quad_kernel, pipes),
        out_shape=jax.ShapeDtypeStruct((batches, tok, width), BF16),
        in_specs=[vmem] * 4 + [far] * 2,
        out_specs=far,
        scratch_shapes=[
            room((2, 2, batches, tok), jnp.int32),
            room((batches, tok), jnp.int32),
            room((batches, tok), F32),
            room((batches, tok, width), BF16),
            room((2, 2, batches, 2, capacity, tok), BF16),
            room((batches, 2, 2, tok, wide), BF16),
            room((batches, tok, wide), BF16),
            room((batches, 2, SLOTS, capacity, wide), BF16),
            room((batches, 2, 2, capacity, wide), BF16),
            room((wide, 2 * units), BF16),
            room((2, 2 * units, wide), BF16),
            room((batches, rows, 2 * units), F32),
            room((batches, rows, 2 * units), BF16),
            room((batches, rows, 2 * units), BF16),
            room((batches, 2, rows, 2 * units), BF16),
            room((batches, rows, wide), BF16),
            room((batches, 2, 2 * capacity, wide), BF16),
            room((batches, tok, 2 * capacity), BF16),
            room((batches, tok, 1), F32),
            room((batches, tok, width), BF16),
            sem((3,)), sem((3,)),
            sem((3,)), sem((3,)),
            sem((batches,)), sem((batches,)),
            sem, sem,
            sem((CHUNKS,)), sem((CHUNKS,)),
            sem((CHUNKS,)), sem((CHUNKS,)),
            sem((CHUNKS,)), sem((CHUNKS,)),
            sem((batches, 2)), sem((batches, 2)),
            sem((batches, 2, SLOTS)), sem((batches, 2, SLOTS)),
            sem((batches, 2, 2)), sem((batches, 2, 2)),
            sem((batches,)), sem((batches,)),
            sem((batches,)), sem((batches,)),
            sem((batches, CHUNKS, 2 * SLOTS)), sem((batches, CHUNKS, 2, 2)),
            sem((2,)),
            sem((batches, CHUNKS, 2)),
        ],
        compiler_params=pltpu.CompilerParams(
            collective_id=1, has_side_effects=True, vmem_limit_bytes=60 * 2**20
        ),
    )(expert_ids[0], activations[0], norm_gain, gate_values[0], up_weight[0], down_weight[0])
    return received[None]


def local(pipes, *arrays):
    if lax.axis_size("expert") == 2 * GROUP:
        return paired(pipes, *arrays)
    return general(pipes, *arrays)


def solution(mesh):
    placed = (
        P("pipe", None, "expert", None),
        P("pipe", None, "expert"),
        P("pipe", None, "expert"),
        P("pipe", None),
        P("pipe", None, "expert"),
        P("pipe", "expert", None),
    )
    return jax.shard_map(
        functools.partial(local, mesh.shape["pipe"]),
        mesh=mesh,
        in_specs=placed,
        out_specs=P("pipe", None, "expert", None),
        check_vma=False,
    )
```

```python
import functools

import jax
import jax.numpy as jnp
from jax import lax
from jax.experimental import pallas as pl
from jax.experimental.pallas import tpu as pltpu
from jax.sharding import PartitionSpec as P

LEVELS = 2


EPSILON = 1e-06
GROUP = 2**LEVELS
MESH = pl.DeviceIdType.MESH
F32, BF16 = jnp.float32, jnp.bfloat16


def remote(source, target, send, recv, **where):
    return pltpu.make_async_remote_copy(
        src_ref=source, dst_ref=target, send_sem=send, recv_sem=recv, device_id=where, device_id_type=MESH
    )


def each(low, high, body):
    def step(index, carry):
        body(index)
        return carry

    lax.fori_loop(low, high, step, 0)


def layer_kernel(
    n, pipes, place, act, gain, gate, up, down, ret, act_out, place_out, gate_out,
    packed, x, up_all, down_all, pres, sums, own_pre, hidden, out,
    usend, urecv, dsend, drecv, psend, precv, xsend, xrecv, ssend, srecv, hsend, hrecv, rsend, rrecv, own,
):
    me, pipe = lax.axis_index("expert"), lax.axis_index("pipe")
    group_index = me // GROUP
    first = group_index * GROUP
    g = me - first
    batches, experts, capacity = place.shape[:3]
    part, units = up.shape[1:]
    ahead, behind = (pipe + 1) % pipes, (pipe + pipes - 1) % pipes
    blocks = n // GROUP
    tall = GROUP * capacity

    barrier = pltpu.get_barrier_semaphore()

    def greet(k):
        pl.semaphore_signal(barrier, inc=1, device_id={"expert": (me + k) % n}, device_id_type=MESH)

    def greet_behind(k):
        pl.semaphore_signal(barrier, inc=1, device_id={"pipe": behind, "expert": k}, device_id_type=MESH)

    each(1, n, greet)
    each(0, n, greet_behind)
    pl.semaphore_wait(barrier, 2 * n - 1)

    def columns(j):
        return pl.ds(pl.multiple_of(j * part, 128), part)

    def share(j):
        return pl.ds(pl.multiple_of(j * units, 128), units)

    def rows_of(d):
        return pl.ds(pl.multiple_of(d * capacity, 16), capacity)

    peers = [(k, (g + k) % GROUP) for k in range(1, GROUP)]
    ups = [remote(up.at[j], up_all.at[g], usend.at[k], urecv.at[k], expert=first + j) for k, j in peers]
    downs = [
        remote(
            down.at[:, columns(j)], down_all.at[share(g), :], dsend.at[k], drecv.at[k], expert=first + j
        )
        for k, j in peers
    ]
    shifts = [
        remote(source, target, psend.at[i], precv.at[i], pipe=ahead)
        for i, (source, target) in enumerate(((act, act_out), (place, place_out), (gate, gate_out)))
    ]

    def dispatch(m, k):
        d = (me + k) % n
        return remote(packed.at[m, d], x.at[m, rows_of(me), :], xsend.at[m, k], xrecv.at[m, k], expert=d)

    for copy in ups:
        copy.start()
    own_up = pltpu.make_async_copy(up.at[g], up_all.at[g], own.at[0])
    own_down = pltpu.make_async_copy(down.at[:, columns(g)], down_all.at[share(g), :], own.at[1])
    own_up.start()
    own_down.start()
    own_rows = []
    for m in range(batches):
        wide = act[m].astype(F32)
        scale = lax.rsqrt(jnp.mean(wide * wide, axis=-1, keepdims=True) + EPSILON)
        normed = (wide * scale * gain[...].astype(F32)).astype(BF16)
        for e in range(experts):
            for j in range(GROUP):
                packed[m, e * GROUP + j] = jnp.dot(
                    place[m, e], normed[:, j * part : (j + 1) * part], preferred_element_type=F32
                ).astype(BF16)
        if m == 0:
            each(1, n, lambda k: dispatch(0, k).start())
        copy = pltpu.make_async_copy(packed.at[m, me], x.at[m, rows_of(me), :], own.at[2 + m])
        copy.start()
        own_rows.append(copy)

    def summing(m, k, j):
        return remote(pres.at[m, k], sums.at[m, k], ssend.at[m, k], srecv.at[m, k], expert=first + j)

    def sharing(m, k, j):
        mine = hidden.at[m, :, share(g)]
        return remote(mine, mine, hsend.at[m, k], hrecv.at[m, k], expert=first + j)

    own_up.wait()
    for copy in ups:
        copy.wait_recv()
    for m in range(batches):
        own_rows[m].wait()
        each(1, n, lambda k, m=m: dispatch(m, k).wait_recv())
        for k, j in peers:
            pres[m, k] = jnp.dot(x[m], up_all[j], preferred_element_type=F32).astype(BF16)
            summing(m, k, j).start()
        if m + 1 < batches:
            each(1, n, lambda k, m=m: dispatch(m + 1, k).start())
        if m == 0:
            for copy in downs + shifts:
                copy.start()
        own_pre[...] = jnp.dot(x[m], up_all[g], preferred_element_type=F32)
        for k, j in peers:
            summing(m, k, j).wait_recv()
        total = own_pre[...]
        for k in range(1, GROUP):
            total = total + sums[m, k].astype(F32)
        hidden[m, :, share(g)] = jax.nn.silu(total).astype(BF16)
        for k, j in peers:
            sharing(m, k, j).start()

    def slots_of(m, source):
        return ret.at[m, rows_of(source // GROUP), columns(source % GROUP)]

    def give(m, target):
        return remote(
            out.at[m, rows_of(target), :], slots_of(m, me), rsend.at[m, target], rrecv.at[m, me],
            pipe=ahead, expert=target,
        )

    own_down.wait()
    for copy in downs:
        copy.wait_recv()
    for m in range(batches):
        for k, j in peers:
            sharing(m, k, j).wait_recv()

        def block(index, m=m):
            owner = (group_index + 1 + index) % blocks
            rows = pl.ds(pl.multiple_of(owner * tall, 16), tall)
            out[m, rows, :] = jnp.dot(
                hidden[m, rows, :], down_all[...], preferred_element_type=F32
            ).astype(BF16)
            for j in range(GROUP):
                give(m, owner * GROUP + j).start()

        each(0, blocks, block)

    for copy in ups + downs:
        copy.wait_send()
    for copy in shifts:
        copy.wait()
    for m in range(batches):
        each(1, n, lambda k, m=m: dispatch(m, k).wait_send())
        for k, j in peers:
            summing(m, k, j).wait_send()
            sharing(m, k, j).wait_send()

        def finish(source, m=m):
            give(m, source).wait_send()
            remote(
                out.at[m, rows_of(source), :], slots_of(m, source), rsend.at[m, source],
                rrecv.at[m, source], pipe=ahead, expert=source,
            ).wait_recv()

        each(0, n, finish)


def general(pipes, activations, expert_ids, gate_values, norm_gain, up_weight, down_weight):
    n = lax.axis_size("expert")
    experts = n // GROUP
    _, batches, tok, width = activations.shape
    part = width // GROUP
    units = up_weight.shape[2]
    capacity = max(2, 3 * tok // (2 * experts))
    capacity = (capacity + 15) // 16 * 16
    rows = n * capacity

    order = jnp.arange(tok, dtype=jnp.int32)
    same = expert_ids[0][:, :, None] == expert_ids[0][:, None, :]
    ranking = jnp.sum((same & (order[None, :] < order[:, None])).astype(jnp.int32), axis=-1)
    slot = expert_ids[0] * capacity + ranking
    slots = jnp.arange(experts * capacity, dtype=jnp.int32).reshape(1, experts, capacity, 1)
    place = (slot[:, None, None, :] == slots).astype(BF16)

    vmem, far = pl.BlockSpec(memory_space=pltpu.VMEM), pl.BlockSpec(memory_space=pl.ANY)
    shape, sem = jax.ShapeDtypeStruct, pltpu.SemaphoreType.DMA
    returned, act_prev, place_prev, gate_prev = pl.pallas_call(
        functools.partial(layer_kernel, n, pipes),
        out_shape=(
            shape((batches, experts * capacity, width), BF16),
            shape((batches, tok, width), BF16),
            shape(place.shape, BF16),
            shape((batches, tok), F32),
        ),
        in_specs=[vmem] * 4 + [far] * 2,
        out_specs=(far,) * 4,
        scratch_shapes=[
            pltpu.VMEM((batches, n, capacity, part), BF16),
            pltpu.VMEM((batches, rows, part), BF16),
            pltpu.VMEM((GROUP, part, units), BF16),
            pltpu.VMEM((GROUP * units, part), BF16),
            pltpu.VMEM((batches, GROUP, rows, units), BF16),
            pltpu.VMEM((batches, GROUP, rows, units), BF16),
            pltpu.VMEM((rows, units), F32),
            pltpu.VMEM((batches, rows, GROUP * units), BF16),
            pltpu.VMEM((batches, rows, part), BF16),
            sem((GROUP,)),
            sem((GROUP,)),
            sem((GROUP,)),
            sem((GROUP,)),
            sem((3,)),
            sem((3,)),
            sem((batches, n)),
            sem((batches, n)),
            sem((batches, GROUP)),
            sem((batches, GROUP)),
            sem((batches, GROUP)),
            sem((batches, GROUP)),
            sem((batches, n)),
            sem((batches, n)),
            sem((2 + batches,)),
        ],
        compiler_params=pltpu.CompilerParams(
            collective_id=0, has_side_effects=True, vmem_limit_bytes=60 * 2**20
        ),
    )(
        place,
        activations[0],
        norm_gain,
        gate_values[0],
        up_weight[0].reshape(GROUP, part, units),
        down_weight[0],
    )

    finished = []
    for m in range(batches):
        expert_out = lax.dot_general(
            place_prev[m].reshape(experts * capacity, tok),
            returned[m],
            (((0,), (0,)), ((), ())),
            preferred_element_type=F32,
        )
        finished.append((act_prev[m].astype(F32) + gate_prev[m][:, None] * expert_out).astype(BF16))
    return jnp.stack(finished)[None]


SLOTS = 4
CHUNKS = 14
EARLY = 9
FIRST = 5
READY = 8
AHEAD = 2
FAR, NEAR, ALL = (2, 2), (0, 2), (0, 4)


def quad_kernel(
    pipes, ids, act, gain, gate, up, down, out,
    ids_all, ids_prev, gate_prev, act_prev, place, dense, halves, x, mixed, wu, wd,
    pre, pre_send, pre_recv, hidden, results, ret, parcels, arrived, spread, gates, final,
    isend, irecv, ssend, srecv, nsend, nrecv, usend, urecv, dsend, drecv, osend, orecv, fsend, frecv,
    gsend, grecv, zsend, zrecv, msend, mrecv, psend, precv, hsend, hrecv, rsend, rrecv, esend, erecv, own, wsem,
):
    me, pipe = lax.axis_index("expert"), lax.axis_index("pipe")
    z, y = me // 2, me % 2
    other = 1 - y
    half = z // 2
    s = (1 - half) * z + half * (3 - z)
    inner, outer = s == 1, s == 0
    batches, tok, width = act.shape
    wide = width // 2
    units = up.shape[1]
    capacity = x.shape[3]
    rows = 2 * SLOTS * capacity
    part = wide // CHUNKS
    block = 2 * capacity
    side = rows // 2
    ahead, behind = (pipe + 1) % pipes, (pipe + pipes - 1) % pipes

    def node(owner, slot, at):
        return ((1 - at) * slot + at * (3 - slot)) * 2 + owner

    beside, across, corner, mate = node(other, s, half), node(y, 1 - s, half), node(other, 1 - s, half), node(y, 1, 1 - half)

    barrier = pltpu.get_barrier_semaphore()

    def greet(**where):
        pl.semaphore_signal(barrier, inc=1, device_id=where, device_id_type=MESH)

    for device in (beside, across, corner):
        greet(expert=device)
    greet(pipe=behind, expert=me)

    @pl.when(inner)
    def _():
        greet(expert=mate)
        greet(pipe=behind, expert=mate)
        pl.semaphore_wait(barrier, 6)

    @pl.when(outer)
    def _():
        pl.semaphore_wait(barrier, 4)

    def wide_half(j):
        return pl.ds(pl.multiple_of(j * wide, 128), wide)

    def piece(c):
        return pl.ds(pl.multiple_of(c * part, 128), part)

    def piece_of(j, c):
        return pl.ds(pl.multiple_of(j * wide + c * part, 128), part)

    def share(j):
        return pl.ds(pl.multiple_of(j * units, 128), units)

    def id_copy(k, device, target):
        return remote(ids, target, isend.at[k], irecv.at[k], expert=device)

    id_out = [id_copy(k, device, ids_all.at[s, y]) for k, device in enumerate((beside, across, corner))]
    id_in = [
        id_copy(0, beside, ids_all.at[s, other]),
        id_copy(1, across, ids_all.at[1 - s, y]),
        id_copy(2, corner, ids_all.at[1 - s, other]),
    ]
    shifts = [
        remote(source, target, ssend.at[i], srecv.at[i], pipe=ahead)
        for i, (source, target) in enumerate(((ids_all, ids_prev), (gate, gate_prev), (act, act_prev)))
    ]

    def swap_rows(m, owner):
        return remote(halves.at[m], dense.at[m, s, owner], nsend.at[m], nrecv.at[m], expert=beside)

    def swap_up(j):
        return remote(up.at[wide_half(other), :], wu.at[:, share(j)], usend, urecv, expert=beside)

    def swap_down(c, j):
        return remote(
            down.at[:, piece_of(other, c)], wd.at[s, share(j), piece(c)], dsend, drecv.at[c], expert=beside
        )

    def lift_down(c):
        return remote(
            down.at[:, piece_of(y, c)], wd.at[0, share(y), piece(c)], osend, orecv.at[c], expert=across
        )

    def pass_down(c):
        block = wd.at[0, share(other), piece(c)]
        return remote(block, block, fsend, frecv.at[c], expert=across)

    def lift_rows(m, owner):
        block = dense.at[m, 0, owner]
        return remote(block, block, gsend.at[m, owner], grecv.at[m, owner], expert=across)

    def drop_rows(m, owner, slot):
        rows_there = x.at[m, slot, owner]
        return remote(rows_there, rows_there, zsend.at[m, owner, slot], zrecv.at[m, owner, slot], expert=across)

    def cross(m, owner, slot):
        return remote(
            mixed.at[m, owner, slot], x.at[m, 3 - slot, owner], msend.at[m, owner, slot],
            mrecv.at[m, owner, slot], expert=mate,
        )

    def lines(slot, count):
        return pl.ds(slot * block, count * block)

    def swap_pre(m, slot, count):
        return remote(
            pre_send.at[m, lines(slot, count)], pre_recv.at[m, lines(slot, count)], psend.at[m, slot],
            precv.at[m, slot], expert=beside,
        )

    def lift_hidden(m, slot, count):
        there = hidden.at[m, 0, lines(slot, count)]
        return remote(there, there, hsend.at[m, slot], hrecv.at[m, slot], expert=across)

    def give(m, c, far):
        where = {"pipe": ahead, "expert": mate if far else me}
        return remote(
            results.at[m, pl.ds(far * side, side), piece(c)], ret.at[m, half, :, piece(c)],
            rsend, rrecv.at[m, c], **where,
        )

    def taken(m, c):
        both = ret.at[m, :, :, piece(c)]
        return remote(both, both, rsend, rrecv.at[m, c], pipe=ahead)

    targets = ((0, other, corner), (0, y, across), (1, other, beside))

    def deliver(m, c, k):
        return remote(
            parcels.at[k, m, :, piece(c)], arrived.at[m, y, :, piece(c)], esend, erecv.at[m, c],
            expert=targets[k][2],
        )

    def delivered(there, m, c):
        return remote(there, there, esend, erecv.at[m, c], expert=beside)

    def written(m, c, j):
        columns = piece_of(j, c)
        return pltpu.make_async_copy(final.at[m, :, columns], out.at[m, :, columns], wsem)

    own_up = pltpu.make_async_copy(up.at[wide_half(y), :], wu.at[:, share(y)], own.at[0])
    own_down = pltpu.make_async_copy(down.at[:, wide_half(y)], wd.at[1, share(y), :], own.at[1])

    for copy in id_out:
        copy.start()
    own_up.start()

    def normalise(m):
        mine = act[m, :, wide_half(y)].astype(F32)
        far = act[m, :, wide_half(other)].astype(F32)
        total = jnp.sum(mine * mine, axis=-1, keepdims=True) + jnp.sum(far * far, axis=-1, keepdims=True)
        scale = lax.rsqrt(total / width + EPSILON)
        halves[m] = (far * scale * gain[:, wide_half(other)].astype(F32)).astype(BF16)
        swap_rows(m, y).start()
        dense[m, s, y] = (mine * scale * gain[:, wide_half(y)].astype(F32)).astype(BF16)

    normalise(0)

    @pl.when(outer)
    def _():
        lift_rows(0, y).start()

    lane = lax.broadcasted_iota(jnp.int32, (tok, tok), 1)
    line = lax.broadcasted_iota(jnp.int32, (tok, tok), 0)
    earlier = (line < lane).astype(BF16)
    later = (lane < line).astype(BF16)
    same = lane == line
    slot_line = lax.broadcasted_iota(jnp.int32, (capacity, tok), 0).astype(F32)
    slot_lane = lax.broadcasted_iota(jnp.int32, (tok, capacity), 1).astype(F32)
    expert_line = lax.broadcasted_iota(jnp.int32, (16, tok), 0)
    expert_lane = lax.broadcasted_iota(jnp.int32, (tok, 128), 1).astype(F32)

    def plan(slot, owner, m):
        onehot = (ids_all[slot, owner, m : m + 1, :] == expert_line).astype(F32)
        before = jnp.dot(onehot.astype(BF16), earlier, preferred_element_type=F32)
        for e in range(2):
            hit = jnp.where(before[e : e + 1] == slot_line, onehot[e : e + 1], 0.0)
            place[slot, owner, m, e] = hit.astype(BF16)

    def plan_back(slot, owner, m):
        line_ids = ids_prev[slot, owner, m : m + 1, :].astype(F32)
        chosen = jnp.sum(jnp.where(same, line_ids, 0.0), axis=1, keepdims=True)
        onehot = (chosen == expert_lane).astype(F32)
        before = jnp.dot(later, onehot.astype(BF16), preferred_element_type=F32)
        rank = jnp.sum(before * onehot, axis=1, keepdims=True)
        for e in range(2):
            spread[slot, owner, m, e] = jnp.where(chosen == e, (rank == slot_lane).astype(F32), 0.0).astype(BF16)

    ids_all[s, y] = ids[...]
    for m in range(batches):
        plan(s, y, m)

    def pack(m, slot, owner, expert):
        return jnp.dot(
            place[slot, owner, m, expert], dense[m, slot, owner], preferred_element_type=F32
        ).astype(BF16)

    def keep(m, slot, owner):
        x[m, slot, owner] = pack(m, slot, owner, half)

    def pack_cross(m, slot, owner):
        mixed[m, owner, slot] = pack(m, slot, owner, 1 - half)
        cross(m, owner, slot).start()

    def pack_inner(m, owner):
        keep(m, 1, owner)
        drop_rows(m, owner, 1).start()
        pack_cross(m, 1, owner)

    def lifted(m, owner):
        lift_rows(m, owner).wait_recv()
        pack_cross(m, 0, owner)
        keep(m, 0, owner)

    def plan_others():
        for copy in id_in:
            copy.wait_recv()
        for copy in shifts:
            copy.start()
        for m in range(batches):
            plan(s, other, m)

    def forward(m, owner, slot):
        cross(m, owner, 3 - slot).wait_recv()
        drop_rows(m, owner, slot).start()

    def partial(m, slot, count):
        total = jnp.dot(
            x[m, slot : slot + count].reshape(count * block, wide), wu[...], preferred_element_type=F32
        )
        pre_send[m, lines(slot, count)] = total.astype(BF16)
        swap_pre(m, slot, count).start()
        pre[m, lines(slot, count)] = total

    def activate(m, slot, count):
        swap_pre(m, slot, count).wait_recv()
        there = lines(slot, count)
        hidden[m, s, there] = jax.nn.silu(pre[m, there] + pre_recv[m, there].astype(F32)).astype(BF16)

    @pl.when(inner)
    def _():
        pack_inner(0, y)
        normalise(1)
        own_down.start()
        plan_others()
        for owner in (y, other):
            for m in range(batches):
                plan(0, owner, m)
        swap_rows(0, other).wait_recv()
        swap_up(y).start()
        swap_down(0, y).start()
        pack_inner(0, other)
        lifted(0, y)
        forward(0, y, 2)
        forward(0, other, 2)
        lifted(0, other)
        pack_cross(1, 1, y)
        swap_rows(1, other).wait_recv()
        pack_cross(1, 1, other)
        forward(0, y, 3)
        lifted(1, y)
        forward(0, other, 3)
        for owner in (y, other):
            keep(1, 1, owner)
        shifts[0].wait_recv()
        for m in range(batches):
            plan_back(0, y, m)
            plan_back(0, other, m)
        lifted(1, other)
        forward(1, y, 2)
        for m in range(batches):
            plan_back(1, y, m)
            plan_back(1, other, m)
        forward(1, other, 2)
        own_up.wait()
        forward(1, y, 3)
        swap_up(other).wait_recv()
        partial(0, *FAR)
        partial(0, *NEAR)
        each(1, FIRST, lambda c: swap_down(c, y).start())
        forward(1, other, 3)
        for owner in (y, other):
            drop_rows(1, owner, 1).start()
        partial(1, *FAR)
        each(FIRST, EARLY, lambda c: swap_down(c, y).start())
        partial(1, *NEAR)
        each(EARLY, CHUNKS, lambda c: swap_down(c, y).start())
        own_down.wait()

    @pl.when(outer)
    def _():
        normalise(1)
        plan_others()
        keep(0, 0, y)
        keep(1, 0, y)
        swap_rows(0, other).wait_recv()
        swap_up(y).start()
        swap_down(0, y).start()
        lift_rows(0, other).start()
        lift_rows(1, y).start()
        keep(0, 0, other)
        swap_rows(1, other).wait_recv()
        lift_rows(1, other).start()
        each(0, READY, lambda c: lift_down(c).start())
        keep(1, 0, other)
        shifts[0].wait_recv()
        own_up.wait()

        def gathered(m, slot, count):
            for k in range(max(slot, 1), slot + count):
                for owner in range(2):
                    drop_rows(m, owner, k).wait_recv()

        def relay(c):
            swap_down(c, other).wait_recv()
            pass_down(c).start()

        def relay_next(c):
            relay(c)
            swap_down(c + AHEAD, y).start()

        def late(c):
            lift_down(c).start()
            relay_next(c)

        def latest(c):
            lift_down(c).start()
            relay(c)

        def raise_hidden(m, slot, count):
            activate(m, slot, count)
            lift_hidden(m, slot, count).start()

        gathered(0, *ALL)
        swap_up(other).wait_recv()
        partial(0, *FAR)
        partial(0, *NEAR)
        each(1, 1 + AHEAD, lambda c: swap_down(c, y).start())
        relay(0)
        raise_hidden(0, *FAR)
        raise_hidden(0, *NEAR)
        each(1, 3, relay_next)
        gathered(1, *FAR)
        partial(1, *FAR)
        each(3, FIRST, relay_next)
        raise_hidden(1, *FAR)
        each(FIRST, READY - 1, relay_next)
        gathered(1, *NEAR)
        partial(1, *NEAR)
        each(READY - 1, READY, relay_next)
        each(READY, EARLY, late)
        raise_hidden(1, *NEAR)
        each(EARLY, CHUNKS - AHEAD, late)
        each(CHUNKS - AHEAD, CHUNKS, latest)

    for copy in shifts[1:]:
        copy.wait_recv()
    for m in range(batches):
        gates[m] = jnp.sum(jnp.where(same, gate_prev[m : m + 1, :], 0.0), axis=1, keepdims=True)

    def await_hidden(m, slot, count):
        activate(m, slot, count)
        lift_hidden(m, slot, count).wait_recv()

    def await_down(c):
        lift_down(c).wait_recv()
        swap_down(c, other).wait_recv()
        pass_down(c).wait_recv()

    def produce(m, c, slot, count):
        there = lines(slot, count)
        total = jnp.dot(hidden[m, 0, there], wd[0, :, piece(c)], preferred_element_type=F32)
        total = total + jnp.dot(hidden[m, 1, there], wd[1, :, piece(c)], preferred_element_type=F32)
        results[m, there, piece(c)] = total.astype(BF16)
        if slot + count == SLOTS:
            give(m, c, 1).start()
        if slot == 0:
            give(m, c, 0).start()

    def combine(m, c):
        taken(m, c).wait_recv()

        def rows_for(slot, owner):
            near = pl.ds(pl.multiple_of((slot * 2 + owner) * capacity, 16), capacity)
            far = pl.ds(pl.multiple_of(((1 - slot) * 2 + owner) * capacity, 16), capacity)
            total = jnp.dot(spread[slot, owner, m, half], ret[m, half, near, piece(c)], preferred_element_type=F32)
            total = total + jnp.dot(
                spread[slot, owner, m, 1 - half], ret[m, 1 - half, far, piece(c)], preferred_element_type=F32
            )
            return total.astype(BF16)

        for k, (slot, owner, _) in enumerate(targets):
            parcels[k, m, :, piece(c)] = rows_for(slot, owner)
            deliver(m, c, k).start()
        arrived[m, y, :, piece(c)] = rows_for(1, y)

    def complete(m, c, j):
        columns = piece_of(j, c)
        final[m, :, columns] = (
            act_prev[m, :, columns].astype(F32) + gates[m] * arrived[m, j, :, piece(c)].astype(F32)
        ).astype(BF16)
        written(m, c, j).start()

    def finish(m, c):
        complete(m, c, y)
        delivered(arrived.at[m, other, :, piece(c)], m, c).wait_recv()
        complete(m, c, other)

    def finish_outer(m, c):
        delivered(arrived.at[m, :, :, piece(c)], m, c).wait_recv()
        for j in range(2):
            complete(m, c, j)

    @pl.when(inner)
    def _():
        await_hidden(0, *FAR)
        await_hidden(0, *NEAR)

        def first(c):
            await_down(c)
            produce(0, c, *ALL)

        each(0, FIRST, first)
        await_hidden(1, *FAR)

        def second(c):
            produce(1, c, *FAR)
            combine(0, c)

        each(0, FIRST, second)

        def third(c):
            await_down(c)
            produce(0, c, *ALL)
            produce(1, c, *FAR)

        each(FIRST, EARLY, third)
        await_hidden(1, *NEAR)
        produce(1, 0, *NEAR)

        def fourth(c):
            produce(1, c, *NEAR)
            combine(1, c - 1)

        def fifth(c):
            produce(1, c, *NEAR)
            combine(0, c)

        each(1, FIRST, fourth)
        each(FIRST, EARLY, fifth)

        def close(c):
            for m in range(batches):
                finish(m, c)

        def join(c):
            for m in range(batches):
                combine(m, c)

        def sixth(c):
            await_down(c)
            produce(0, c, *ALL)
            produce(1, c, *ALL)
            combine(1, c - FIRST)

        lag = CHUNKS - EARLY - 2

        def seventh(c):
            sixth(c)
            close(c - EARLY)

        def eighth(c):
            sixth(c)
            join(c - lag)
            close(lag + 2 * (c - EARLY - lag))
            close(lag + 2 * (c - EARLY - lag) + 1)

        each(EARLY, EARLY + lag, seventh)
        each(EARLY + lag, CHUNKS, eighth)

        def ninth(c):
            join(c)
            close(c - lag - 1)

        each(CHUNKS - lag, CHUNKS, ninth)
        each(CHUNKS - lag - 1, CHUNKS, close)

    @pl.when(outer)
    def _():
        each(0, EARLY, lambda c: finish_outer(0, c))
        each(0, EARLY, lambda c: finish_outer(1, c))

        def rest(c):
            for m in range(batches):
                finish_outer(m, c)

        each(EARLY, CHUNKS, rest)

    for copy in id_out + shifts:
        copy.wait_send()
    swap_up(y).wait_send()
    remote(down.at[:, wide_half(other)], wd.at[s, share(y), :], dsend, drecv.at[0], expert=beside).wait_send()
    for m in range(batches):
        swap_rows(m, y).wait_send()
        for group in (FAR, NEAR):
            swap_pre(m, *group).wait_send()

    @pl.when(inner)
    def _():
        for m in range(batches):
            for owner in range(2):
                for slot in range(1, SLOTS):
                    drop_rows(m, owner, slot).wait_send()
                for slot in range(2):
                    cross(m, owner, slot).wait_send()
        remote(results, results, rsend, rrecv.at[0, 0], pipe=ahead).wait_send()
        remote(parcels, parcels, esend, erecv.at[0, 0], expert=beside).wait_send()

    @pl.when(outer)
    def _():
        for m in range(batches):
            for group in (FAR, NEAR):
                lift_hidden(m, *group).wait_send()
            for owner in range(2):
                lift_rows(m, owner).wait_send()
        moved = wd.at[0, share(y), :]
        remote(moved, moved, osend, orecv.at[0], expert=across).wait_send()
        remote(moved, moved, fsend, frecv.at[0], expert=across).wait_send()

    pltpu.make_async_copy(final, out, wsem).wait()


def paired(pipes, activations, expert_ids, gate_values, norm_gain, up_weight, down_weight):
    _, batches, tok, width = activations.shape
    wide = width // 2
    units = up_weight.shape[2]
    capacity = (3 * tok // 4 + 15) // 16 * 16
    rows = 2 * SLOTS * capacity
    vmem, far = pl.BlockSpec(memory_space=pltpu.VMEM), pl.BlockSpec(memory_space=pl.ANY)
    room, sem = pltpu.VMEM, pltpu.SemaphoreType.DMA
    received = pl.pallas_call(
        functools.partial(quad_kernel, pipes),
        out_shape=jax.ShapeDtypeStruct((batches, tok, width), BF16),
        in_specs=[vmem] * 4 + [far] * 2,
        out_specs=far,
        scratch_shapes=[
            room((2, 2, batches, tok), jnp.int32),
            room((2, 2, batches, tok), jnp.int32),
            room((batches, tok), F32),
            room((batches, tok, width), BF16),
            room((2, 2, batches, 2, capacity, tok), BF16),
            room((batches, 2, 2, tok, wide), BF16),
            room((batches, tok, wide), BF16),
            room((batches, SLOTS, 2, capacity, wide), BF16),
            room((batches, 2, 2, capacity, wide), BF16),
            room((wide, 2 * units), BF16),
            room((2, 2 * units, wide), BF16),
            room((batches, rows, 2 * units), F32),
            room((batches, rows, 2 * units), BF16),
            room((batches, rows, 2 * units), BF16),
            room((batches, 2, rows, 2 * units), BF16),
            room((batches, rows, wide), BF16),
            room((batches, 2, rows // 2, wide), BF16),
            room((3, batches, tok, wide), BF16),
            room((batches, 2, tok, wide), BF16),
            room((2, 2, batches, 2, tok, capacity), BF16),
            room((batches, tok, 1), F32),
            room((batches, tok, width), BF16),
            sem((3,)), sem((3,)),
            sem((3,)), sem((3,)),
            sem((batches,)), sem((batches,)),
            sem, sem,
            sem, sem((CHUNKS,)),
            sem, sem((CHUNKS,)),
            sem, sem((CHUNKS,)),
            sem((batches, 2)), sem((batches, 2)),
            sem((batches, 2, SLOTS)), sem((batches, 2, SLOTS)),
            sem((batches, 2, 2)), sem((batches, 2, 2)),
            sem((batches, SLOTS)), sem((batches, SLOTS)),
            sem((batches, SLOTS)), sem((batches, SLOTS)),
            sem, sem((batches, CHUNKS)),
            sem, sem((batches, CHUNKS)),
            sem((2,)),
            sem,
        ],
        compiler_params=pltpu.CompilerParams(
            collective_id=1, has_side_effects=True, vmem_limit_bytes=60 * 2**20
        ),
    )(expert_ids[0], activations[0], norm_gain, gate_values[0], up_weight[0], down_weight[0])
    return received[None]


def local(pipes, *arrays):
    if lax.axis_size("expert") == 2 * GROUP:
        return paired(pipes, *arrays)
    return general(pipes, *arrays)


def solution(mesh):
    placed = (
        P("pipe", None, "expert", None),
        P("pipe", None, "expert"),
        P("pipe", None, "expert"),
        P("pipe", None),
        P("pipe", None, "expert"),
        P("pipe", "expert", None),
    )
    return jax.shard_map(
        functools.partial(local, mesh.shape["pipe"]),
        mesh=mesh,
        in_specs=placed,
        out_specs=P("pipe", None, "expert", None),
        check_vma=False,
    )
```

```python
import functools

import jax
import jax.numpy as jnp
from jax import lax
from jax.experimental import pallas as pl
from jax.experimental.pallas import tpu as pltpu
from jax.sharding import PartitionSpec as P

LEVELS = 2


EPSILON = 1e-06
GROUP = 2**LEVELS
MESH = pl.DeviceIdType.MESH
F32, BF16 = jnp.float32, jnp.bfloat16


def remote(source, target, send, recv, **where):
    return pltpu.make_async_remote_copy(
        src_ref=source, dst_ref=target, send_sem=send, recv_sem=recv, device_id=where, device_id_type=MESH
    )


def each(low, high, body):
    def step(index, carry):
        body(index)
        return carry

    lax.fori_loop(low, high, step, 0)


def layer_kernel(
    n, pipes, place, act, gain, gate, up, down, ret, act_out, place_out, gate_out,
    packed, x, up_all, down_all, pres, sums, own_pre, hidden, out,
    usend, urecv, dsend, drecv, psend, precv, xsend, xrecv, ssend, srecv, hsend, hrecv, rsend, rrecv, own,
):
    me, pipe = lax.axis_index("expert"), lax.axis_index("pipe")
    group_index = me // GROUP
    first = group_index * GROUP
    g = me - first
    batches, experts, capacity = place.shape[:3]
    part, units = up.shape[1:]
    ahead, behind = (pipe + 1) % pipes, (pipe + pipes - 1) % pipes
    blocks = n // GROUP
    tall = GROUP * capacity

    barrier = pltpu.get_barrier_semaphore()

    def greet(k):
        pl.semaphore_signal(barrier, inc=1, device_id={"expert": (me + k) % n}, device_id_type=MESH)

    def greet_behind(k):
        pl.semaphore_signal(barrier, inc=1, device_id={"pipe": behind, "expert": k}, device_id_type=MESH)

    each(1, n, greet)
    each(0, n, greet_behind)
    pl.semaphore_wait(barrier, 2 * n - 1)

    def columns(j):
        return pl.ds(pl.multiple_of(j * part, 128), part)

    def share(j):
        return pl.ds(pl.multiple_of(j * units, 128), units)

    def rows_of(d):
        return pl.ds(pl.multiple_of(d * capacity, 16), capacity)

    peers = [(k, (g + k) % GROUP) for k in range(1, GROUP)]
    ups = [remote(up.at[j], up_all.at[g], usend.at[k], urecv.at[k], expert=first + j) for k, j in peers]
    downs = [
        remote(
            down.at[:, columns(j)], down_all.at[share(g), :], dsend.at[k], drecv.at[k], expert=first + j
        )
        for k, j in peers
    ]
    shifts = [
        remote(source, target, psend.at[i], precv.at[i], pipe=ahead)
        for i, (source, target) in enumerate(((act, act_out), (place, place_out), (gate, gate_out)))
    ]

    def dispatch(m, k):
        d = (me + k) % n
        return remote(packed.at[m, d], x.at[m, rows_of(me), :], xsend.at[m, k], xrecv.at[m, k], expert=d)

    for copy in ups:
        copy.start()
    own_up = pltpu.make_async_copy(up.at[g], up_all.at[g], own.at[0])
    own_down = pltpu.make_async_copy(down.at[:, columns(g)], down_all.at[share(g), :], own.at[1])
    own_up.start()
    own_down.start()
    own_rows = []
    for m in range(batches):
        wide = act[m].astype(F32)
        scale = lax.rsqrt(jnp.mean(wide * wide, axis=-1, keepdims=True) + EPSILON)
        normed = (wide * scale * gain[...].astype(F32)).astype(BF16)
        for e in range(experts):
            for j in range(GROUP):
                packed[m, e * GROUP + j] = jnp.dot(
                    place[m, e], normed[:, j * part : (j + 1) * part], preferred_element_type=F32
                ).astype(BF16)
        if m == 0:
            each(1, n, lambda k: dispatch(0, k).start())
        copy = pltpu.make_async_copy(packed.at[m, me], x.at[m, rows_of(me), :], own.at[2 + m])
        copy.start()
        own_rows.append(copy)

    def summing(m, k, j):
        return remote(pres.at[m, k], sums.at[m, k], ssend.at[m, k], srecv.at[m, k], expert=first + j)

    def sharing(m, k, j):
        mine = hidden.at[m, :, share(g)]
        return remote(mine, mine, hsend.at[m, k], hrecv.at[m, k], expert=first + j)

    own_up.wait()
    for copy in ups:
        copy.wait_recv()
    for m in range(batches):
        own_rows[m].wait()
        each(1, n, lambda k, m=m: dispatch(m, k).wait_recv())
        for k, j in peers:
            pres[m, k] = jnp.dot(x[m], up_all[j], preferred_element_type=F32).astype(BF16)
            summing(m, k, j).start()
        if m + 1 < batches:
            each(1, n, lambda k, m=m: dispatch(m + 1, k).start())
        if m == 0:
            for copy in downs + shifts:
                copy.start()
        own_pre[...] = jnp.dot(x[m], up_all[g], preferred_element_type=F32)
        for k, j in peers:
            summing(m, k, j).wait_recv()
        total = own_pre[...]
        for k in range(1, GROUP):
            total = total + sums[m, k].astype(F32)
        hidden[m, :, share(g)] = jax.nn.silu(total).astype(BF16)
        for k, j in peers:
            sharing(m, k, j).start()

    def slots_of(m, source):
        return ret.at[m, rows_of(source // GROUP), columns(source % GROUP)]

    def give(m, target):
        return remote(
            out.at[m, rows_of(target), :], slots_of(m, me), rsend.at[m, target], rrecv.at[m, me],
            pipe=ahead, expert=target,
        )

    own_down.wait()
    for copy in downs:
        copy.wait_recv()
    for m in range(batches):
        for k, j in peers:
            sharing(m, k, j).wait_recv()

        def block(index, m=m):
            owner = (group_index + 1 + index) % blocks
            rows = pl.ds(pl.multiple_of(owner * tall, 16), tall)
            out[m, rows, :] = jnp.dot(
                hidden[m, rows, :], down_all[...], preferred_element_type=F32
            ).astype(BF16)
            for j in range(GROUP):
                give(m, owner * GROUP + j).start()

        each(0, blocks, block)

    for copy in ups + downs:
        copy.wait_send()
    for copy in shifts:
        copy.wait()
    for m in range(batches):
        each(1, n, lambda k, m=m: dispatch(m, k).wait_send())
        for k, j in peers:
            summing(m, k, j).wait_send()
            sharing(m, k, j).wait_send()

        def finish(source, m=m):
            give(m, source).wait_send()
            remote(
                out.at[m, rows_of(source), :], slots_of(m, source), rsend.at[m, source],
                rrecv.at[m, source], pipe=ahead, expert=source,
            ).wait_recv()

        each(0, n, finish)


def general(pipes, activations, expert_ids, gate_values, norm_gain, up_weight, down_weight):
    n = lax.axis_size("expert")
    experts = n // GROUP
    _, batches, tok, width = activations.shape
    part = width // GROUP
    units = up_weight.shape[2]
    capacity = max(2, 3 * tok // (2 * experts))
    capacity = (capacity + 15) // 16 * 16
    rows = n * capacity

    order = jnp.arange(tok, dtype=jnp.int32)
    same = expert_ids[0][:, :, None] == expert_ids[0][:, None, :]
    ranking = jnp.sum((same & (order[None, :] < order[:, None])).astype(jnp.int32), axis=-1)
    slot = expert_ids[0] * capacity + ranking
    slots = jnp.arange(experts * capacity, dtype=jnp.int32).reshape(1, experts, capacity, 1)
    place = (slot[:, None, None, :] == slots).astype(BF16)

    vmem, far = pl.BlockSpec(memory_space=pltpu.VMEM), pl.BlockSpec(memory_space=pl.ANY)
    shape, sem = jax.ShapeDtypeStruct, pltpu.SemaphoreType.DMA
    returned, act_prev, place_prev, gate_prev = pl.pallas_call(
        functools.partial(layer_kernel, n, pipes),
        out_shape=(
            shape((batches, experts * capacity, width), BF16),
            shape((batches, tok, width), BF16),
            shape(place.shape, BF16),
            shape((batches, tok), F32),
        ),
        in_specs=[vmem] * 4 + [far] * 2,
        out_specs=(far,) * 4,
        scratch_shapes=[
            pltpu.VMEM((batches, n, capacity, part), BF16),
            pltpu.VMEM((batches, rows, part), BF16),
            pltpu.VMEM((GROUP, part, units), BF16),
            pltpu.VMEM((GROUP * units, part), BF16),
            pltpu.VMEM((batches, GROUP, rows, units), BF16),
            pltpu.VMEM((batches, GROUP, rows, units), BF16),
            pltpu.VMEM((rows, units), F32),
            pltpu.VMEM((batches, rows, GROUP * units), BF16),
            pltpu.VMEM((batches, rows, part), BF16),
            sem((GROUP,)),
            sem((GROUP,)),
            sem((GROUP,)),
            sem((GROUP,)),
            sem((3,)),
            sem((3,)),
            sem((batches, n)),
            sem((batches, n)),
            sem((batches, GROUP)),
            sem((batches, GROUP)),
            sem((batches, GROUP)),
            sem((batches, GROUP)),
            sem((batches, n)),
            sem((batches, n)),
            sem((2 + batches,)),
        ],
        compiler_params=pltpu.CompilerParams(
            collective_id=0, has_side_effects=True, vmem_limit_bytes=60 * 2**20
        ),
    )(
        place,
        activations[0],
        norm_gain,
        gate_values[0],
        up_weight[0].reshape(GROUP, part, units),
        down_weight[0],
    )

    finished = []
    for m in range(batches):
        expert_out = lax.dot_general(
            place_prev[m].reshape(experts * capacity, tok),
            returned[m],
            (((0,), (0,)), ((), ())),
            preferred_element_type=F32,
        )
        finished.append((act_prev[m].astype(F32) + gate_prev[m][:, None] * expert_out).astype(BF16))
    return jnp.stack(finished)[None]


SLOTS = 4
CHUNKS = 14
EARLY = 8
FIRST = 6
AHEAD = 2
FAR, NEAR, ALL = (2, 2), (0, 2), (0, 4)


def quad_kernel(
    pipes, ids, gain, gate, source, up, down, out,
    act, ids_all, ids_prev, gate_prev, act_prev, place, dense, halves, x, mixed, wu, wd,
    pre, pre_send, pre_recv, hidden, results, ret, parcels, arrived, spread, gates,
    isend, irecv, ssend, srecv, nsend, nrecv, usend, urecv, dsend, drecv, osend, fsend, frecv,
    gsend, grecv, zsend, zrecv, msend, mrecv, psend, precv, hsend, hrecv, rsend, rrecv, esend, erecv, own,
):
    me, pipe = lax.axis_index("expert"), lax.axis_index("pipe")
    z, y = me // 2, me % 2
    other = 1 - y
    half = z // 2
    s = (1 - half) * z + half * (3 - z)
    inner, outer = s == 1, s == 0
    batches, tok, width = act.shape
    wide = width // 2
    units = up.shape[1]
    capacity = x.shape[3]
    rows = 2 * SLOTS * capacity
    part = wide // CHUNKS
    block = 2 * capacity
    side = rows // 2
    ahead, behind = (pipe + 1) % pipes, (pipe + pipes - 1) % pipes

    def node(owner, slot, at):
        return ((1 - at) * slot + at * (3 - slot)) * 2 + owner

    beside, across, corner, mate = node(other, s, half), node(y, 1 - s, half), node(other, 1 - s, half), node(y, 1, 1 - half)

    loads = [pltpu.make_async_copy(source.at[m], act.at[m], own.at[2 + m]) for m in range(batches)]
    for copy in loads:
        copy.start()
    barrier = pltpu.get_barrier_semaphore()

    def greet(**where):
        pl.semaphore_signal(barrier, inc=1, device_id=where, device_id_type=MESH)

    for device in (beside, across, corner):
        greet(expert=device)
    greet(pipe=behind, expert=me)

    @pl.when(inner)
    def _():
        greet(expert=mate)
        greet(pipe=behind, expert=mate)
        pl.semaphore_wait(barrier, 6)

    @pl.when(outer)
    def _():
        pl.semaphore_wait(barrier, 4)

    def wide_half(j):
        return pl.ds(pl.multiple_of(j * wide, 128), wide)

    def piece(c):
        return pl.ds(pl.multiple_of(c * part, 128), part)

    def piece_of(j, c):
        return pl.ds(pl.multiple_of(j * wide + c * part, 128), part)

    def share(j):
        return pl.ds(pl.multiple_of(j * units, 128), units)

    def id_copy(k, device, target):
        return remote(ids, target, isend.at[k], irecv.at[k], expert=device)

    id_out = [id_copy(k, device, ids_all.at[s, y]) for k, device in enumerate((beside, across, corner))]
    id_in = [
        id_copy(0, beside, ids_all.at[s, other]),
        id_copy(1, across, ids_all.at[1 - s, y]),
        id_copy(2, corner, ids_all.at[1 - s, other]),
    ]
    shifts = [
        remote(source, target, ssend.at[i], srecv.at[i], pipe=ahead)
        for i, (source, target) in enumerate(((ids_all, ids_prev), (gate, gate_prev), (source, act_prev)))
    ]

    def swap_rows(m, owner):
        return remote(halves.at[m], dense.at[m, s, owner], nsend, nrecv.at[m], expert=beside)

    def swap_up(j):
        return remote(up.at[wide_half(other), :], wu.at[:, share(j)], usend, urecv, expert=beside)

    def swap_down(c, j):
        return remote(
            down.at[:, piece_of(other, c)], wd.at[s, share(j), piece(c)], dsend, drecv.at[c], expert=beside
        )

    def lift_down(c):
        return remote(
            down.at[:, piece_of(y, c)], wd.at[0, share(y), piece(c)], osend, frecv.at[c], expert=across
        )

    def pass_down(c):
        block = wd.at[0, share(other), piece(c)]
        return remote(block, block, fsend, frecv.at[c], expert=across)

    def lift_rows(m, owner):
        block = dense.at[m, 0, owner]
        return remote(block, block, gsend, grecv.at[m, owner], expert=across)

    def drop_rows(m, owner, slot):
        rows_there = x.at[m, slot, owner]
        return remote(rows_there, rows_there, zsend, zrecv.at[m, slot // 2], expert=across)

    def cross(m, owner, slot):
        return remote(
            mixed.at[m, owner, slot], x.at[m, 3 - slot, owner], msend,
            mrecv.at[m, owner, slot], expert=mate,
        )

    def lines(slot, count):
        return pl.ds(slot * block, count * block)

    def swap_pre(m, slot, count):
        return remote(
            pre_send.at[m, lines(slot, count)], pre_recv.at[m, lines(slot, count)], psend,
            precv.at[m, slot // 2], expert=beside,
        )

    def lift_hidden(m, slot, count):
        there = hidden.at[m, 0, lines(slot, count)]
        return remote(there, there, hsend, hrecv.at[m, slot // 2], expert=across)

    def give(m, c, far):
        where = {"pipe": ahead, "expert": mate if far else me}
        return remote(
            results.at[m, pl.ds(far * side, side), piece(c)], ret.at[m, half, :, piece(c)],
            rsend, rrecv.at[m, c], **where,
        )

    def taken(m, c):
        both = ret.at[m, :, :, piece(c)]
        return remote(both, both, rsend, rrecv.at[m, c], pipe=ahead)

    targets = ((0, other, corner), (0, y, across), (1, other, beside))

    def deliver(m, c, k):
        return remote(
            parcels.at[k, m, :, piece(c)], arrived.at[m, y, :, piece(c)], esend, erecv.at[m, c],
            expert=targets[k][2],
        )

    def delivered(there, m, c):
        return remote(there, there, esend, erecv.at[m, c], expert=beside)

    own_up = pltpu.make_async_copy(up.at[wide_half(y), :], wu.at[:, share(y)], own.at[0])
    own_down = pltpu.make_async_copy(down.at[:, wide_half(y)], wd.at[1, share(y), :], own.at[1])

    for copy in id_out:
        copy.start()
    own_up.start()

    def normalise(m):
        loads[m].wait()
        mine = act[m, :, wide_half(y)].astype(F32)
        far = act[m, :, wide_half(other)].astype(F32)
        total = jnp.sum(mine * mine, axis=-1, keepdims=True) + jnp.sum(far * far, axis=-1, keepdims=True)
        scale = lax.rsqrt(total / width + EPSILON)
        halves[m] = (far * scale * gain[:, wide_half(other)].astype(F32)).astype(BF16)
        swap_rows(m, y).start()
        dense[m, s, y] = (mine * scale * gain[:, wide_half(y)].astype(F32)).astype(BF16)

    normalise(0)

    @pl.when(outer)
    def _():
        lift_rows(0, y).start()

    lane = lax.broadcasted_iota(jnp.int32, (tok, tok), 1)
    line = lax.broadcasted_iota(jnp.int32, (tok, tok), 0)
    earlier = (line < lane).astype(BF16)
    later = (lane < line).astype(BF16)
    same = lane == line
    slot_line = lax.broadcasted_iota(jnp.int32, (capacity, tok), 0).astype(F32)
    slot_lane = lax.broadcasted_iota(jnp.int32, (tok, capacity), 1).astype(F32)
    expert_line = lax.broadcasted_iota(jnp.int32, (16, tok), 0)
    expert_lane = lax.broadcasted_iota(jnp.int32, (tok, 128), 1).astype(F32)

    def plan(slot, owner, m):
        onehot = (ids_all[slot, owner, m : m + 1, :] == expert_line).astype(F32)
        before = jnp.dot(onehot.astype(BF16), earlier, preferred_element_type=F32)
        for e in range(2):
            hit = jnp.where(before[e : e + 1] == slot_line, onehot[e : e + 1], 0.0)
            place[slot, owner, m, e] = hit.astype(BF16)

    def plan_back(slot, owner, m):
        line_ids = ids_prev[slot, owner, m : m + 1, :].astype(F32)
        chosen = jnp.sum(jnp.where(same, line_ids, 0.0), axis=1, keepdims=True)
        onehot = (chosen == expert_lane).astype(F32)
        before = jnp.dot(later, onehot.astype(BF16), preferred_element_type=F32)
        rank = jnp.sum(before * onehot, axis=1, keepdims=True)
        for e in range(2):
            spread[slot, owner, m, e] = jnp.where(chosen == e, (rank == slot_lane).astype(F32), 0.0).astype(BF16)

    ids_all[s, y] = ids[...]
    for m in range(batches):
        plan(s, y, m)

    def pack(m, slot, owner, expert):
        return jnp.dot(
            place[slot, owner, m, expert], dense[m, slot, owner], preferred_element_type=F32
        ).astype(BF16)

    def keep(m, slot, owner):
        x[m, slot, owner] = pack(m, slot, owner, half)

    def pack_cross(m, slot, owner):
        mixed[m, owner, slot] = pack(m, slot, owner, 1 - half)
        cross(m, owner, slot).start()

    def pack_inner(m, owner):
        keep(m, 1, owner)
        drop_rows(m, owner, 1).start()
        pack_cross(m, 1, owner)

    def lifted(m, owner):
        lift_rows(m, owner).wait_recv()
        pack_cross(m, 0, owner)
        keep(m, 0, owner)

    def plan_others():
        for copy in id_in:
            copy.wait_recv()
        for copy in shifts:
            copy.start()
        for m in range(batches):
            plan(s, other, m)

    def forward(m, owner, slot):
        cross(m, owner, 3 - slot).wait_recv()
        drop_rows(m, owner, slot).start()

    def partial(m, slot, count):
        total = jnp.dot(
            x[m, slot : slot + count].reshape(count * block, wide), wu[...], preferred_element_type=F32
        )
        pre_send[m, lines(slot, count)] = total.astype(BF16)
        swap_pre(m, slot, count).start()
        pre[m, lines(slot, count)] = total

    def activate(m, slot, count):
        swap_pre(m, slot, count).wait_recv()
        there = lines(slot, count)
        hidden[m, s, there] = jax.nn.silu(pre[m, there] + pre_recv[m, there].astype(F32)).astype(BF16)

    @pl.when(inner)
    def _():
        pack_inner(0, y)
        normalise(1)
        own_down.start()
        plan_others()
        for owner in (y, other):
            for m in range(batches):
                plan(0, owner, m)
        swap_rows(0, other).wait_recv()
        swap_up(y).start()
        swap_down(0, y).start()
        pack_inner(0, other)
        lifted(0, y)
        forward(0, y, 2)
        forward(0, other, 2)
        lifted(0, other)
        pack_cross(1, 1, y)
        swap_rows(1, other).wait_recv()
        pack_cross(1, 1, other)
        forward(0, y, 3)
        lifted(1, y)
        forward(0, other, 3)
        for owner in (y, other):
            keep(1, 1, owner)
        shifts[0].wait_recv()
        for m in range(batches):
            plan_back(0, y, m)
            plan_back(0, other, m)
        lifted(1, other)
        forward(1, y, 2)
        for m in range(batches):
            plan_back(1, y, m)
            plan_back(1, other, m)
        forward(1, other, 2)
        own_up.wait()
        forward(1, y, 3)
        swap_up(other).wait_recv()
        partial(0, *FAR)
        each(1, FIRST, lambda c: swap_down(c, y).start())
        forward(1, other, 3)
        for owner in (y, other):
            drop_rows(1, owner, 1).start()
        partial(1, *FAR)
        partial(0, *NEAR)
        each(FIRST, EARLY, lambda c: swap_down(c, y).start())
        partial(1, *NEAR)
        each(EARLY, CHUNKS, lambda c: swap_down(c, y).start())
        own_down.wait()

    @pl.when(outer)
    def _():
        normalise(1)
        plan_others()
        keep(0, 0, y)
        keep(1, 0, y)
        swap_rows(0, other).wait_recv()
        swap_up(y).start()
        swap_down(0, y).start()
        lift_rows(0, other).start()
        lift_rows(1, y).start()
        keep(0, 0, other)
        swap_rows(1, other).wait_recv()
        lift_rows(1, other).start()
        each(0, EARLY, lambda c: lift_down(c).start())
        keep(1, 0, other)
        shifts[0].wait_recv()
        own_up.wait()

        def gathered(m, slot, count):
            if slot + count == SLOTS:
                both = x.at[m, pl.ds(2, 2)]
                remote(both, both, zsend, zrecv.at[m, 1], expert=across).wait_recv()
            if slot == 0:
                remote(x.at[m, 1], x.at[m, 1], zsend, zrecv.at[m, 0], expert=across).wait_recv()

        def relay(c):
            swap_down(c, other).wait_recv()
            pass_down(c).start()

        def relay_next(c):
            relay(c)
            swap_down(c + AHEAD, y).start()

        def late(c):
            lift_down(c).start()
            relay_next(c)

        def latest(c):
            lift_down(c).start()
            relay(c)

        def raise_hidden(m, slot, count):
            activate(m, slot, count)
            lift_hidden(m, slot, count).start()

        gathered(0, *ALL)
        swap_up(other).wait_recv()
        partial(0, *FAR)
        each(1, 1 + AHEAD, lambda c: swap_down(c, y).start())
        relay(0)
        raise_hidden(0, *FAR)
        each(1, FIRST - AHEAD, relay_next)
        relay(FIRST - AHEAD)
        gathered(1, *FAR)
        partial(1, *FAR)
        partial(0, *NEAR)
        swap_down(FIRST, y).start()
        relay_next(FIRST - 1)
        raise_hidden(1, *FAR)
        raise_hidden(0, *NEAR)
        relay(FIRST)
        gathered(1, *NEAR)
        partial(1, *NEAR)
        swap_down(FIRST + AHEAD, y).start()
        relay_next(FIRST + 1)
        raise_hidden(1, *NEAR)
        each(EARLY, CHUNKS - AHEAD, late)
        each(CHUNKS - AHEAD, CHUNKS, latest)

    for copy in shifts[1:]:
        copy.wait_recv()
    for m in range(batches):
        gates[m] = jnp.sum(jnp.where(same, gate_prev[m : m + 1, :], 0.0), axis=1, keepdims=True)

    def await_hidden(m, slot, count):
        activate(m, slot, count)
        lift_hidden(m, slot, count).wait_recv()

    def await_down(c):
        swap_down(c, other).wait_recv()
        both = wd.at[0, :, piece(c)]
        remote(both, both, fsend, frecv.at[c], expert=across).wait_recv()

    def produce(m, c, slot, count):
        there = lines(slot, count)
        total = jnp.dot(hidden[m, 0, there], wd[0, :, piece(c)], preferred_element_type=F32)
        total = total + jnp.dot(hidden[m, 1, there], wd[1, :, piece(c)], preferred_element_type=F32)
        results[m, there, piece(c)] = total.astype(BF16)
        if slot + count == SLOTS:
            give(m, c, 1).start()
        if slot == 0:
            give(m, c, 0).start()

    def combine(m, c):
        taken(m, c).wait_recv()

        def rows_for(slot, owner):
            near = pl.ds(pl.multiple_of((slot * 2 + owner) * capacity, 16), capacity)
            far = pl.ds(pl.multiple_of(((1 - slot) * 2 + owner) * capacity, 16), capacity)
            total = jnp.dot(spread[slot, owner, m, half], ret[m, half, near, piece(c)], preferred_element_type=F32)
            total = total + jnp.dot(
                spread[slot, owner, m, 1 - half], ret[m, 1 - half, far, piece(c)], preferred_element_type=F32
            )
            return total.astype(BF16)

        for k, (slot, owner, _) in enumerate(targets):
            parcels[k, m, :, piece(c)] = rows_for(slot, owner)
            deliver(m, c, k).start()
        arrived[m, y, :, piece(c)] = rows_for(1, y)

    def complete(m, c, j):
        columns = piece_of(j, c)
        out[m, :, columns] = (
            act_prev[m, :, columns].astype(F32) + gates[m] * arrived[m, j, :, piece(c)].astype(F32)
        ).astype(BF16)

    def finish(m, c):
        complete(m, c, y)
        delivered(arrived.at[m, other, :, piece(c)], m, c).wait_recv()
        complete(m, c, other)

    def finish_outer(m, c):
        delivered(arrived.at[m, :, :, piece(c)], m, c).wait_recv()
        for j in range(2):
            complete(m, c, j)

    @pl.when(inner)
    def _():
        def close(c):
            for m in range(batches):
                finish(m, c)

        def join(c):
            for m in range(batches):
                combine(m, c)

        def first(c):
            await_down(c)
            produce(0, c, *FAR)

        def third(c):
            await_down(c)
            produce(0, c, *ALL)
            produce(1, c, *FAR)

        def late(c):
            await_down(c)
            produce(0, c, *ALL)
            produce(1, c, *ALL)

        def fifth(c):
            late(c)
            join(c - 2)
            for i in range(2):
                close(2 * (c - EARLY - 1) + i)

        await_hidden(0, *FAR)
        each(0, FIRST, first)
        await_hidden(1, *FAR)
        each(0, FIRST, lambda c: produce(1, c, *FAR))
        await_hidden(0, *NEAR)
        each(0, FIRST, lambda c: produce(0, c, *NEAR))
        third(FIRST)
        each(0, 2, lambda c: combine(0, c))
        third(FIRST + 1)
        each(2, FIRST - 1, lambda c: combine(0, c))
        await_hidden(1, *NEAR)
        each(0, EARLY, lambda c: produce(1, c, *NEAR))
        combine(0, FIRST - 1)
        each(0, FIRST - 2, lambda c: combine(1, c))
        late(EARLY)
        each(FIRST - 2, FIRST, lambda c: combine(1, c))
        join(FIRST)
        each(EARLY + 1, CHUNKS, fifth)
        join(CHUNKS - 2)
        each(2 * (CHUNKS - EARLY - 1), CHUNKS - 3, close)
        join(CHUNKS - 1)
        each(CHUNKS - 3, CHUNKS, close)

    @pl.when(outer)
    def _():
        each(0, EARLY, lambda c: finish_outer(0, c))
        each(0, EARLY, lambda c: finish_outer(1, c))

        def rest(c):
            for m in range(batches):
                finish_outer(m, c)

        each(EARLY, CHUNKS, rest)

    for copy in id_out + shifts:
        copy.wait_send()
    swap_up(y).wait_send()
    remote(down.at[:, wide_half(other)], wd.at[s, share(y), :], dsend, drecv.at[0], expert=beside).wait_send()

    def all_sent(whole, sent):
        remote(whole, whole, sent, frecv.at[0], expert=beside).wait_send()

    all_sent(halves, nsend)
    all_sent(pre_send, psend)

    @pl.when(inner)
    def _():
        all_sent(x.at[:, pl.ds(1, 3)], zsend)
        all_sent(mixed, msend)
        all_sent(results, rsend)
        all_sent(parcels, esend)

    @pl.when(outer)
    def _():
        all_sent(hidden.at[:, 0], hsend)
        all_sent(dense.at[:, 0], gsend)
        moved = wd.at[0, share(y), :]
        all_sent(moved, osend)
        all_sent(moved, fsend)


def paired(pipes, activations, expert_ids, gate_values, norm_gain, up_weight, down_weight):
    _, batches, tok, width = activations.shape
    wide = width // 2
    units = up_weight.shape[2]
    capacity = (3 * tok // 4 + 15) // 16 * 16
    rows = 2 * SLOTS * capacity
    vmem, far = pl.BlockSpec(memory_space=pltpu.VMEM), pl.BlockSpec(memory_space=pl.ANY)
    room, sem = pltpu.VMEM, pltpu.SemaphoreType.DMA
    received = pl.pallas_call(
        functools.partial(quad_kernel, pipes),
        out_shape=pltpu.VMEM((batches, tok, width), BF16),
        in_specs=[vmem] * 3 + [far] * 3,
        out_specs=vmem,
        scratch_shapes=[
            room((batches, tok, width), BF16),
            room((2, 2, batches, tok), jnp.int32),
            room((2, 2, batches, tok), jnp.int32),
            room((batches, tok), F32),
            room((batches, tok, width), BF16),
            room((2, 2, batches, 2, capacity, tok), BF16),
            room((batches, 2, 2, tok, wide), BF16),
            room((batches, tok, wide), BF16),
            room((batches, SLOTS, 2, capacity, wide), BF16),
            room((batches, 2, 2, capacity, wide), BF16),
            room((wide, 2 * units), BF16),
            room((2, 2 * units, wide), BF16),
            room((batches, rows, 2 * units), F32),
            room((batches, rows, 2 * units), BF16),
            room((batches, rows, 2 * units), BF16),
            room((batches, 2, rows, 2 * units), BF16),
            room((batches, rows, wide), BF16),
            room((batches, 2, rows // 2, wide), BF16),
            room((3, batches, tok, wide), BF16),
            room((batches, 2, tok, wide), BF16),
            room((2, 2, batches, 2, tok, capacity), BF16),
            room((batches, tok, 1), F32),
            sem((3,)), sem((3,)),
            sem((3,)), sem((3,)),
            sem, sem((batches,)),
            sem, sem,
            sem, sem((CHUNKS,)),
            sem, sem, sem((CHUNKS,)),
            sem, sem((batches, 2)),
            sem, sem((batches, 2)),
            sem, sem((batches, 2, 2)),
            sem, sem((batches, 2)),
            sem, sem((batches, 2)),
            sem, sem((batches, CHUNKS)),
            sem, sem((batches, CHUNKS)),
            sem((2 + batches,)),
        ],
        compiler_params=pltpu.CompilerParams(
            collective_id=1, has_side_effects=True, vmem_limit_bytes=56 * 2**20
        ),
    )(expert_ids[0], norm_gain, gate_values[0], activations[0], up_weight[0], down_weight[0])
    return received[None]


def local(pipes, *arrays):
    if lax.axis_size("expert") == 2 * GROUP:
        return paired(pipes, *arrays)
    return general(pipes, *arrays)


def solution(mesh):
    placed = (
        P("pipe", None, "expert", None),
        P("pipe", None, "expert"),
        P("pipe", None, "expert"),
        P("pipe", None),
        P("pipe", None, "expert"),
        P("pipe", "expert", None),
    )
    return jax.shard_map(
        functools.partial(local, mesh.shape["pipe"]),
        mesh=mesh,
        in_specs=placed,
        out_specs=P("pipe", None, "expert", None),
        check_vma=False,
    )
```

```python
import functools

import jax
import jax.numpy as jnp
from jax import lax
from jax.experimental import pallas as pl
from jax.experimental.pallas import tpu as pltpu
from jax.sharding import PartitionSpec as P

LEVELS = 2


EPSILON = 1e-06
GROUP = 2**LEVELS
MESH = pl.DeviceIdType.MESH
F32, BF16 = jnp.float32, jnp.bfloat16


def remote(source, target, send, recv, **where):
    return pltpu.make_async_remote_copy(
        src_ref=source, dst_ref=target, send_sem=send, recv_sem=recv, device_id=where, device_id_type=MESH
    )


def each(low, high, body):
    def step(index, carry):
        body(index)
        return carry

    lax.fori_loop(low, high, step, 0)


def layer_kernel(
    n, pipes, place, act, gain, gate, up, down, ret, act_out, place_out, gate_out,
    packed, x, up_all, down_all, pres, sums, own_pre, hidden, out,
    usend, urecv, dsend, drecv, psend, precv, xsend, xrecv, ssend, srecv, hsend, hrecv, rsend, rrecv, own,
):
    me, pipe = lax.axis_index("expert"), lax.axis_index("pipe")
    group_index = me // GROUP
    first = group_index * GROUP
    g = me - first
    batches, experts, capacity = place.shape[:3]
    part, units = up.shape[1:]
    ahead, behind = (pipe + 1) % pipes, (pipe + pipes - 1) % pipes
    blocks = n // GROUP
    tall = GROUP * capacity

    barrier = pltpu.get_barrier_semaphore()

    def greet(k):
        pl.semaphore_signal(barrier, inc=1, device_id={"expert": (me + k) % n}, device_id_type=MESH)

    def greet_behind(k):
        pl.semaphore_signal(barrier, inc=1, device_id={"pipe": behind, "expert": k}, device_id_type=MESH)

    each(1, n, greet)
    each(0, n, greet_behind)
    pl.semaphore_wait(barrier, 2 * n - 1)

    def columns(j):
        return pl.ds(pl.multiple_of(j * part, 128), part)

    def share(j):
        return pl.ds(pl.multiple_of(j * units, 128), units)

    def rows_of(d):
        return pl.ds(pl.multiple_of(d * capacity, 16), capacity)

    peers = [(k, (g + k) % GROUP) for k in range(1, GROUP)]
    ups = [remote(up.at[j], up_all.at[g], usend.at[k], urecv.at[k], expert=first + j) for k, j in peers]
    downs = [
        remote(
            down.at[:, columns(j)], down_all.at[share(g), :], dsend.at[k], drecv.at[k], expert=first + j
        )
        for k, j in peers
    ]
    shifts = [
        remote(source, target, psend.at[i], precv.at[i], pipe=ahead)
        for i, (source, target) in enumerate(((act, act_out), (place, place_out), (gate, gate_out)))
    ]

    def dispatch(m, k):
        d = (me + k) % n
        return remote(packed.at[m, d], x.at[m, rows_of(me), :], xsend.at[m, k], xrecv.at[m, k], expert=d)

    for copy in ups:
        copy.start()
    own_up = pltpu.make_async_copy(up.at[g], up_all.at[g], own.at[0])
    own_down = pltpu.make_async_copy(down.at[:, columns(g)], down_all.at[share(g), :], own.at[1])
    own_up.start()
    own_down.start()
    own_rows = []
    for m in range(batches):
        wide = act[m].astype(F32)
        scale = lax.rsqrt(jnp.mean(wide * wide, axis=-1, keepdims=True) + EPSILON)
        normed = (wide * scale * gain[...].astype(F32)).astype(BF16)
        for e in range(experts):
            for j in range(GROUP):
                packed[m, e * GROUP + j] = jnp.dot(
                    place[m, e], normed[:, j * part : (j + 1) * part], preferred_element_type=F32
                ).astype(BF16)
        if m == 0:
            each(1, n, lambda k: dispatch(0, k).start())
        copy = pltpu.make_async_copy(packed.at[m, me], x.at[m, rows_of(me), :], own.at[2 + m])
        copy.start()
        own_rows.append(copy)

    def summing(m, k, j):
        return remote(pres.at[m, k], sums.at[m, k], ssend.at[m, k], srecv.at[m, k], expert=first + j)

    def sharing(m, k, j):
        mine = hidden.at[m, :, share(g)]
        return remote(mine, mine, hsend.at[m, k], hrecv.at[m, k], expert=first + j)

    own_up.wait()
    for copy in ups:
        copy.wait_recv()
    for m in range(batches):
        own_rows[m].wait()
        each(1, n, lambda k, m=m: dispatch(m, k).wait_recv())
        for k, j in peers:
            pres[m, k] = jnp.dot(x[m], up_all[j], preferred_element_type=F32).astype(BF16)
            summing(m, k, j).start()
        if m + 1 < batches:
            each(1, n, lambda k, m=m: dispatch(m + 1, k).start())
        if m == 0:
            for copy in downs + shifts:
                copy.start()
        own_pre[...] = jnp.dot(x[m], up_all[g], preferred_element_type=F32)
        for k, j in peers:
            summing(m, k, j).wait_recv()
        total = own_pre[...]
        for k in range(1, GROUP):
            total = total + sums[m, k].astype(F32)
        hidden[m, :, share(g)] = jax.nn.silu(total).astype(BF16)
        for k, j in peers:
            sharing(m, k, j).start()

    def slots_of(m, source):
        return ret.at[m, rows_of(source // GROUP), columns(source % GROUP)]

    def give(m, target):
        return remote(
            out.at[m, rows_of(target), :], slots_of(m, me), rsend.at[m, target], rrecv.at[m, me],
            pipe=ahead, expert=target,
        )

    own_down.wait()
    for copy in downs:
        copy.wait_recv()
    for m in range(batches):
        for k, j in peers:
            sharing(m, k, j).wait_recv()

        def block(index, m=m):
            owner = (group_index + 1 + index) % blocks
            rows = pl.ds(pl.multiple_of(owner * tall, 16), tall)
            out[m, rows, :] = jnp.dot(
                hidden[m, rows, :], down_all[...], preferred_element_type=F32
            ).astype(BF16)
            for j in range(GROUP):
                give(m, owner * GROUP + j).start()

        each(0, blocks, block)

    for copy in ups + downs:
        copy.wait_send()
    for copy in shifts:
        copy.wait()
    for m in range(batches):
        each(1, n, lambda k, m=m: dispatch(m, k).wait_send())
        for k, j in peers:
            summing(m, k, j).wait_send()
            sharing(m, k, j).wait_send()

        def finish(source, m=m):
            give(m, source).wait_send()
            remote(
                out.at[m, rows_of(source), :], slots_of(m, source), rsend.at[m, source],
                rrecv.at[m, source], pipe=ahead, expert=source,
            ).wait_recv()

        each(0, n, finish)


def general(pipes, activations, expert_ids, gate_values, norm_gain, up_weight, down_weight):
    n = lax.axis_size("expert")
    experts = n // GROUP
    _, batches, tok, width = activations.shape
    part = width // GROUP
    units = up_weight.shape[2]
    capacity = max(2, 3 * tok // (2 * experts))
    capacity = (capacity + 15) // 16 * 16
    rows = n * capacity

    order = jnp.arange(tok, dtype=jnp.int32)
    same = expert_ids[0][:, :, None] == expert_ids[0][:, None, :]
    ranking = jnp.sum((same & (order[None, :] < order[:, None])).astype(jnp.int32), axis=-1)
    slot = expert_ids[0] * capacity + ranking
    slots = jnp.arange(experts * capacity, dtype=jnp.int32).reshape(1, experts, capacity, 1)
    place = (slot[:, None, None, :] == slots).astype(BF16)

    vmem, far = pl.BlockSpec(memory_space=pltpu.VMEM), pl.BlockSpec(memory_space=pl.ANY)
    shape, sem = jax.ShapeDtypeStruct, pltpu.SemaphoreType.DMA
    returned, act_prev, place_prev, gate_prev = pl.pallas_call(
        functools.partial(layer_kernel, n, pipes),
        out_shape=(
            shape((batches, experts * capacity, width), BF16),
            shape((batches, tok, width), BF16),
            shape(place.shape, BF16),
            shape((batches, tok), F32),
        ),
        in_specs=[vmem] * 4 + [far] * 2,
        out_specs=(far,) * 4,
        scratch_shapes=[
            pltpu.VMEM((batches, n, capacity, part), BF16),
            pltpu.VMEM((batches, rows, part), BF16),
            pltpu.VMEM((GROUP, part, units), BF16),
            pltpu.VMEM((GROUP * units, part), BF16),
            pltpu.VMEM((batches, GROUP, rows, units), BF16),
            pltpu.VMEM((batches, GROUP, rows, units), BF16),
            pltpu.VMEM((rows, units), F32),
            pltpu.VMEM((batches, rows, GROUP * units), BF16),
            pltpu.VMEM((batches, rows, part), BF16),
            sem((GROUP,)),
            sem((GROUP,)),
            sem((GROUP,)),
            sem((GROUP,)),
            sem((3,)),
            sem((3,)),
            sem((batches, n)),
            sem((batches, n)),
            sem((batches, GROUP)),
            sem((batches, GROUP)),
            sem((batches, GROUP)),
            sem((batches, GROUP)),
            sem((batches, n)),
            sem((batches, n)),
            sem((2 + batches,)),
        ],
        compiler_params=pltpu.CompilerParams(
            collective_id=0, has_side_effects=True, vmem_limit_bytes=60 * 2**20
        ),
    )(
        place,
        activations[0],
        norm_gain,
        gate_values[0],
        up_weight[0].reshape(GROUP, part, units),
        down_weight[0],
    )

    finished = []
    for m in range(batches):
        expert_out = lax.dot_general(
            place_prev[m].reshape(experts * capacity, tok),
            returned[m],
            (((0,), (0,)), ((), ())),
            preferred_element_type=F32,
        )
        finished.append((act_prev[m].astype(F32) + gate_prev[m][:, None] * expert_out).astype(BF16))
    return jnp.stack(finished)[None]


SLOTS = 4
CHUNKS = 14
EARLY = 8
FIRST = 6
AHEAD = 2
FAR, NEAR, ALL = (2, 2), (0, 2), (0, 4)


def quad_kernel(
    pipes, ids, gain, gate, source, up, down, out,
    act, ids_all, ids_prev, gate_prev, act_prev, place, dense, halves, x, mixed, wu, wd,
    pre, pre_send, pre_recv, hidden, results, ret, parcels, arrived, spread, gates,
    isend, irecv, ssend, srecv, nsend, nrecv, usend, urecv, dsend, drecv, osend, fsend, frecv,
    gsend, grecv, zsend, zrecv, msend, mrecv, psend, precv, hsend, hrecv, ksend, krecv, rsend, rrecv, esend, erecv, own,
):
    me, pipe = lax.axis_index("expert"), lax.axis_index("pipe")
    z, y = me // 2, me % 2
    other = 1 - y
    half = z // 2
    s = (1 - half) * z + half * (3 - z)
    inner, outer = s == 1, s == 0
    batches, tok, width = act.shape
    wide = width // 2
    units = up.shape[1]
    capacity = x.shape[3]
    rows = 2 * SLOTS * capacity
    part = wide // CHUNKS
    block = 2 * capacity
    ahead, behind = (pipe + 1) % pipes, (pipe + pipes - 1) % pipes

    def node(owner, slot, at):
        return ((1 - at) * slot + at * (3 - slot)) * 2 + owner

    beside, across, corner, mate = node(other, s, half), node(y, 1 - s, half), node(other, 1 - s, half), node(y, 1, 1 - half)

    loads = [pltpu.make_async_copy(source.at[m], act.at[m], own.at[2 + m]) for m in range(batches)]
    for copy in loads:
        copy.start()
    barrier = pltpu.get_barrier_semaphore()

    def greet(**where):
        pl.semaphore_signal(barrier, inc=1, device_id=where, device_id_type=MESH)

    for device in (beside, across, corner):
        greet(expert=device)
    greet(pipe=behind, expert=me)

    @pl.when(inner)
    def _():
        greet(expert=mate)
        greet(pipe=behind, expert=mate)
        pl.semaphore_wait(barrier, 6)

    @pl.when(outer)
    def _():
        pl.semaphore_wait(barrier, 4)

    def wide_half(j):
        return pl.ds(pl.multiple_of(j * wide, 128), wide)

    def span(c):
        return c if isinstance(c, tuple) else (c, c * part, part)

    def double(k):
        return 2 * k, 2 * k * part, 2 * part

    def piece(c):
        _, start, size = span(c)
        return pl.ds(pl.multiple_of(start, 128), size)

    def piece_of(j, c):
        _, start, size = span(c)
        return pl.ds(pl.multiple_of(j * wide + start, 128), size)

    def share(j):
        return pl.ds(pl.multiple_of(j * units, 128), units)

    def id_copy(k, device, target):
        return remote(ids, target, isend.at[k], irecv.at[k], expert=device)

    id_out = [id_copy(k, device, ids_all.at[s, y]) for k, device in enumerate((beside, across, corner))]
    id_in = [
        id_copy(0, beside, ids_all.at[s, other]),
        id_copy(1, across, ids_all.at[1 - s, y]),
        id_copy(2, corner, ids_all.at[1 - s, other]),
    ]
    shifts = [
        remote(source, target, ssend.at[i], srecv.at[i], pipe=ahead)
        for i, (source, target) in enumerate(((ids_all, ids_prev), (gate, gate_prev), (source, act_prev)))
    ]

    def swap_rows(m, owner):
        return remote(halves.at[m], dense.at[m, s, owner], nsend, nrecv.at[m], expert=beside)

    def swap_up(j):
        return remote(up.at[wide_half(other), :], wu.at[:, share(j)], usend, urecv, expert=beside)

    def swap_down(c, j):
        return remote(
            down.at[:, piece_of(other, c)], wd.at[s, share(j), piece(c)], dsend, drecv.at[c], expert=beside
        )

    def lift_down(c):
        return remote(
            down.at[:, piece_of(y, c)], wd.at[0, share(y), piece(c)], osend, frecv.at[c], expert=across
        )

    def pass_down(c):
        block = wd.at[0, share(other), piece(c)]
        return remote(block, block, fsend, frecv.at[c], expert=across)

    def lift_rows(m, owner):
        block = dense.at[m, 0, owner]
        return remote(block, block, gsend, grecv.at[m, owner], expert=across)

    def drop_rows(m, owner, slot):
        rows_there = x.at[m, slot, owner]
        return remote(rows_there, rows_there, zsend, zrecv.at[m, slot // 2], expert=across)

    def cross(m, owner, slot):
        return remote(
            mixed.at[m, owner, slot], x.at[m, 2 + slot, owner], msend,
            mrecv.at[m, owner, slot], expert=mate,
        )

    def lines(slot, count):
        return pl.ds(slot * block, count * block)

    def swap_pre(m, slot, count):
        return remote(
            pre_send.at[m, lines(slot, count)], pre_recv.at[m, lines(slot, count)], psend,
            precv.at[m, slot // 2], expert=beside,
        )

    def lift_hidden(m, slot, count):
        if slot:
            there = hidden.at[m, 0, pl.ds(slot, count)]
            return remote(there, there, hsend, hrecv.at[m, 1], expert=across)
        there = hidden.at[m, 0, pl.ds(0, count), y]
        return remote(there, there, ksend, hrecv.at[m, 0], expert=across)

    def share_hidden(m, owner):
        there = hidden.at[m, 0, pl.ds(0, 2), owner]
        return remote(there, there, ksend, krecv.at[m], expert=beside)

    def give(m, c, far):
        where = {"pipe": ahead, "expert": mate if far else me}
        return remote(
            results.at[m, pl.ds(far * SLOTS, SLOTS), :, piece(c)], ret.at[m, :, half, :, piece(c)],
            rsend, rrecv.at[m, c], **where,
        )

    def taken(m, c):
        both = ret.at[m, :, :, :, piece(c)]
        return remote(both, both, rsend, rrecv.at[m, c], pipe=ahead)

    targets = ((0, other, corner), (0, y, across), (1, other, beside))

    def deliver(m, c, k):
        return remote(
            parcels.at[k, m, :, piece(c)], arrived.at[m, y, :, piece(c)], esend, erecv.at[m, span(c)[0]],
            expert=targets[k][2],
        )

    def delivered(there, m, c):
        return remote(there, there, esend, erecv.at[m, span(c)[0]], expert=beside)

    own_up = pltpu.make_async_copy(up.at[wide_half(y), :], wu.at[:, share(y)], own.at[0])
    own_down = pltpu.make_async_copy(down.at[:, wide_half(y)], wd.at[1, share(y), :], own.at[1])

    for copy in id_out:
        copy.start()
    own_up.start()

    def normalise(m):
        loads[m].wait()
        mine = act[m, :, wide_half(y)].astype(F32)
        far = act[m, :, wide_half(other)].astype(F32)
        total = jnp.sum(mine * mine, axis=-1, keepdims=True) + jnp.sum(far * far, axis=-1, keepdims=True)
        scale = lax.rsqrt(total / width + EPSILON)
        halves[m] = (far * scale * gain[:, wide_half(other)].astype(F32)).astype(BF16)
        swap_rows(m, y).start()
        dense[m, s, y] = (mine * scale * gain[:, wide_half(y)].astype(F32)).astype(BF16)

    normalise(0)

    @pl.when(outer)
    def _():
        lift_rows(0, y).start()
        lift_down(0).start()

    lane = lax.broadcasted_iota(jnp.int32, (tok, tok), 1)
    line = lax.broadcasted_iota(jnp.int32, (tok, tok), 0)
    earlier = (line < lane).astype(BF16)
    later = (lane < line).astype(BF16)
    same = lane == line
    slot_line = lax.broadcasted_iota(jnp.int32, (capacity, tok), 0).astype(F32)
    slot_lane = lax.broadcasted_iota(jnp.int32, (tok, block), 1).astype(F32)
    expert_line = lax.broadcasted_iota(jnp.int32, (16, tok), 0)
    expert_lane = lax.broadcasted_iota(jnp.int32, (tok, 128), 1).astype(F32)

    def plan(slot, owner, m):
        onehot = (ids_all[slot, owner, m : m + 1, :] == expert_line).astype(F32)
        before = jnp.dot(onehot.astype(BF16), earlier, preferred_element_type=F32)
        for e in range(2):
            hit = jnp.where(before[e : e + 1] == slot_line, onehot[e : e + 1], 0.0)
            place[slot, owner, m, e] = hit.astype(BF16)

    def plan_back(slot, owner, m):
        line_ids = ids_prev[slot, owner, m : m + 1, :].astype(F32)
        chosen = jnp.sum(jnp.where(same, line_ids, 0.0), axis=1, keepdims=True)
        onehot = (chosen == expert_lane).astype(F32)
        before = jnp.dot(later, onehot.astype(BF16), preferred_element_type=F32)
        rank = jnp.sum(before * onehot, axis=1, keepdims=True)
        spread[slot, owner, m] = (chosen * capacity + rank == slot_lane).astype(BF16)

    ids_all[s, y] = ids[...]
    for m in range(batches):
        plan(s, y, m)

    def pack(m, slot, owner, expert):
        return jnp.dot(
            place[slot, owner, m, expert], dense[m, slot, owner], preferred_element_type=F32
        ).astype(BF16)

    def keep(m, slot, owner):
        x[m, slot, owner] = pack(m, slot, owner, half)

    def pack_cross(m, slot, owner):
        mixed[m, owner, slot] = pack(m, slot, owner, 1 - half)
        cross(m, owner, slot).start()

    def pack_inner(m, owner):
        keep(m, 1, owner)
        drop_rows(m, owner, 1).start()
        pack_cross(m, 1, owner)

    def lifted(m, owner):
        lift_rows(m, owner).wait_recv()
        pack_cross(m, 0, owner)
        keep(m, 0, owner)

    def plan_others():
        for copy in id_in:
            copy.wait_recv()
        for copy in shifts:
            copy.start()
        for m in range(batches):
            plan(s, other, m)

    def forward(m, owner, slot):
        cross(m, owner, slot - 2).wait_recv()
        drop_rows(m, owner, slot).start()

    def partial(m, slot, count):
        total = jnp.dot(
            x[m, slot : slot + count].reshape(count * block, wide), wu[...], preferred_element_type=F32
        )
        pre_send[m, lines(slot, count)] = total.astype(BF16)
        swap_pre(m, slot, count).start()
        pre[m, lines(slot, count)] = total

    def activate(m, slot, count):
        swap_pre(m, slot, count).wait_recv()
        there = lines(slot, count)
        value = jax.nn.silu(pre[m, there] + pre_recv[m, there].astype(F32)).astype(BF16)
        hidden[m, s, pl.ds(slot, count)] = value.reshape(count, 2, capacity, 2 * units)

    @pl.when(inner)
    def _():
        pack_inner(0, y)
        normalise(1)
        own_down.start()
        plan_others()
        for owner in (y, other):
            for m in range(batches):
                plan(0, owner, m)
        swap_rows(0, other).wait_recv()
        swap_up(y).start()
        swap_down(0, y).start()
        pack_inner(0, other)
        lifted(0, y)
        forward(0, y, 3)
        forward(0, other, 3)
        lifted(0, other)
        pack_cross(1, 1, y)
        swap_rows(1, other).wait_recv()
        pack_cross(1, 1, other)
        forward(0, y, 2)
        lifted(1, y)
        forward(0, other, 2)
        for owner in (y, other):
            keep(1, 1, owner)
        shifts[0].wait_recv()
        for m in range(batches):
            plan_back(0, y, m)
            plan_back(0, other, m)
        lifted(1, other)
        forward(1, y, 3)
        for m in range(batches):
            plan_back(1, y, m)
            plan_back(1, other, m)
        forward(1, other, 3)
        own_up.wait()
        forward(1, y, 2)
        swap_up(other).wait_recv()
        partial(0, *FAR)
        each(1, FIRST, lambda c: swap_down(c, y).start())
        forward(1, other, 2)
        for owner in (y, other):
            drop_rows(1, owner, 1).start()
        partial(1, *FAR)
        partial(0, *NEAR)
        swap_down(FIRST, y).start()
        own_down.wait()

    @pl.when(outer)
    def _():
        normalise(1)
        plan_others()
        keep(0, 0, y)
        keep(1, 0, y)
        swap_rows(0, other).wait_recv()
        swap_up(y).start()
        swap_down(0, y).start()
        lift_rows(0, other).start()
        lift_rows(1, y).start()
        keep(0, 0, other)
        swap_rows(1, other).wait_recv()
        lift_rows(1, other).start()
        each(1, EARLY + 1, lambda c: lift_down(c).start())
        keep(1, 0, other)
        shifts[0].wait_recv()
        own_up.wait()

        def gathered(m, slot, count):
            if slot + count == SLOTS:
                both = x.at[m, pl.ds(2, 2)]
                remote(both, both, zsend, zrecv.at[m, 1], expert=across).wait_recv()
            if slot == 0:
                remote(x.at[m, 1], x.at[m, 1], zsend, zrecv.at[m, 0], expert=across).wait_recv()

        def relay(c):
            swap_down(c, other).wait_recv()
            pass_down(c).start()

        def relay_next(c):
            relay(c)
            swap_down(c + AHEAD, y).start()

        def late(c):
            lift_down(c + 1).start()
            relay_next(c)


        def raise_hidden(m, slot, count):
            activate(m, slot, count)
            lift_hidden(m, slot, count).start()

        gathered(0, *ALL)
        swap_up(other).wait_recv()
        partial(0, *FAR)
        each(1, 1 + AHEAD, lambda c: swap_down(c, y).start())
        relay(0)
        raise_hidden(0, *FAR)
        each(1, FIRST - AHEAD, relay_next)
        relay(FIRST - AHEAD)
        gathered(1, *FAR)
        partial(1, *FAR)
        partial(0, *NEAR)
        swap_down(FIRST, y).start()
        relay_next(FIRST - 1)
        raise_hidden(1, *FAR)
        raise_hidden(0, *NEAR)
        relay(FIRST)
        gathered(1, *NEAR)
        partial(1, *NEAR)
        swap_down(FIRST + AHEAD, y).start()
        relay_next(FIRST + 1)
        raise_hidden(1, *NEAR)
        each(EARLY, CHUNKS - AHEAD, late)
        lift_down(CHUNKS - 1).start()
        each(CHUNKS - AHEAD, CHUNKS, relay)

    for copy in shifts[1:]:
        copy.wait_recv()
    for m in range(batches):
        gates[m] = jnp.sum(jnp.where(same, gate_prev[m : m + 1, :], 0.0), axis=1, keepdims=True)

    def await_hidden(m, slot, count):
        activate(m, slot, count)
        lift_hidden(m, slot, count).wait_recv()
        if slot == 0:
            share_hidden(m, y).start()

    def await_down(c):
        swap_down(c, other).wait_recv()
        both = wd.at[0, :, piece(c)]
        remote(both, both, fsend, frecv.at[c], expert=across).wait_recv()

    def produce(m, c, slot, count):
        def of(side):
            there = hidden[m, side, pl.ds(slot, count)].reshape(count * block, 2 * units)
            return jnp.dot(there, wd[side, :, piece(c)], preferred_element_type=F32)

        total = of(0) + of(1)
        results[m, pl.ds(2 * slot, 2 * count), :, piece(c)] = total.astype(BF16).reshape(2 * count, capacity, part)
        if slot + count == SLOTS:
            give(m, c, 1).start()
        if slot == 0:
            give(m, c, 0).start()

    def combine(m, c):
        index, _, size = span(c)
        for i in range(size // part):
            taken(m, index + i).wait_recv()

        def rows_for(slot, owner):
            there = ret[m, 2 * slot + owner, :, :, piece(c)].reshape(block, size)
            return jnp.dot(spread[slot, owner, m], there, preferred_element_type=F32).astype(BF16)

        for k, (slot, owner, _) in enumerate(targets):
            parcels[k, m, :, piece(c)] = rows_for(slot, owner)
            deliver(m, c, k).start()
        arrived[m, y, :, piece(c)] = rows_for(1, y)

    def complete(m, c, j):
        columns = piece_of(j, c)
        out[m, :, columns] = (
            act_prev[m, :, columns].astype(F32) + gates[m] * arrived[m, j, :, piece(c)].astype(F32)
        ).astype(BF16)

    def finish(m, c):
        complete(m, c, y)
        delivered(arrived.at[m, other, :, piece(c)], m, c).wait_recv()
        complete(m, c, other)

    def finish_outer(m, c):
        delivered(arrived.at[m, :, :, piece(c)], m, c).wait_recv()
        for j in range(2):
            complete(m, c, j)

    @pl.when(inner)
    def _():
        def close(c):
            for m in range(batches):
                finish(m, c)

        def join(c):
            for m in range(batches):
                combine(m, c)

        def first(c):
            await_down(c)
            produce(0, c, *FAR)

        def third(c):
            await_down(c)
            produce(0, c, *ALL)
            produce(1, c, *FAR)

        def late(c):
            await_down(c)
            produce(0, c, *ALL)
            produce(1, c, *ALL)

        await_hidden(0, *FAR)
        each(0, FIRST, first)
        await_hidden(1, *FAR)
        each(0, FIRST, lambda c: produce(1, c, *FAR))
        await_hidden(0, *NEAR)
        swap_down(FIRST + 1, y).start()
        partial(1, *NEAR)
        swap_down(EARLY, y).start()
        share_hidden(0, other).wait_recv()
        each(0, FIRST, lambda c: produce(0, c, *NEAR))
        third(FIRST)
        combine(0, double(0))
        third(FIRST + 1)
        combine(0, double(1))
        await_hidden(1, *NEAR)
        each(EARLY + 1, CHUNKS, lambda c: swap_down(c, y).start())
        third(EARLY)
        combine(0, double(2))
        share_hidden(1, other).wait_recv()
        each(0, EARLY + 1, lambda c: produce(1, c, *NEAR))
        combine(1, double(0))
        late(EARLY + 1)
        each(1, 3, lambda k: combine(1, double(k)))
        join(double(3))
        late(EARLY + 2)
        join(EARLY)
        close(double(0))
        late(EARLY + 3)
        join(EARLY + 1)
        close(double(1))
        late(EARLY + 4)
        join(EARLY + 2)
        close(double(2))
        late(EARLY + 5)
        close(double(3))
        join(EARLY + 3)
        close(EARLY)
        join(EARLY + 4)
        each(EARLY + 1, EARLY + 4, close)
        join(EARLY + 5)
        each(EARLY + 4, CHUNKS, close)

    @pl.when(outer)
    def _():
        for m in range(batches):
            each(0, EARLY // 2, lambda k, m=m: finish_outer(m, double(k)))

        def rest(c):
            for m in range(batches):
                finish_outer(m, c)

        each(EARLY, CHUNKS, rest)

    for copy in id_out + shifts:
        copy.wait_send()
    swap_up(y).wait_send()
    remote(down.at[:, wide_half(other)], wd.at[s, share(y), :], dsend, drecv.at[0], expert=beside).wait_send()

    def all_sent(whole, sent):
        remote(whole, whole, sent, frecv.at[0], expert=beside).wait_send()

    all_sent(halves, nsend)
    all_sent(hidden.at[:, 0, pl.ds(0, 2), y], ksend)
    all_sent(pre_send, psend)

    @pl.when(inner)
    def _():
        all_sent(x.at[:, pl.ds(1, 3)], zsend)
        all_sent(mixed, msend)
        all_sent(results, rsend)
        all_sent(parcels, esend)

    @pl.when(outer)
    def _():
        all_sent(hidden.at[:, 0, pl.ds(2, 2)], hsend)
        all_sent(dense.at[:, 0], gsend)
        moved = wd.at[0, share(y), :]
        all_sent(moved, osend)
        all_sent(moved, fsend)


def paired(pipes, activations, expert_ids, gate_values, norm_gain, up_weight, down_weight):
    _, batches, tok, width = activations.shape
    wide = width // 2
    units = up_weight.shape[2]
    capacity = (3 * tok // 4 + 15) // 16 * 16
    rows = 2 * SLOTS * capacity
    vmem, far = pl.BlockSpec(memory_space=pltpu.VMEM), pl.BlockSpec(memory_space=pl.ANY)
    room, sem = pltpu.VMEM, pltpu.SemaphoreType.DMA
    received = pl.pallas_call(
        functools.partial(quad_kernel, pipes),
        out_shape=pltpu.VMEM((batches, tok, width), BF16),
        in_specs=[vmem] * 3 + [far] * 3,
        out_specs=vmem,
        scratch_shapes=[
            room((batches, tok, width), BF16),
            room((2, 2, batches, tok), jnp.int32),
            room((2, 2, batches, tok), jnp.int32),
            room((batches, tok), F32),
            room((batches, tok, width), BF16),
            room((2, 2, batches, 2, capacity, tok), BF16),
            room((batches, 2, 2, tok, wide), BF16),
            room((batches, tok, wide), BF16),
            room((batches, SLOTS, 2, capacity, wide), BF16),
            room((batches, 2, 2, capacity, wide), BF16),
            room((wide, 2 * units), BF16),
            room((2, 2 * units, wide), BF16),
            room((batches, rows, 2 * units), F32),
            room((batches, rows, 2 * units), BF16),
            room((batches, rows, 2 * units), BF16),
            room((batches, 2, SLOTS, 2, capacity, 2 * units), BF16),
            room((batches, 2 * SLOTS, capacity, wide), BF16),
            room((batches, SLOTS, 2, capacity, wide), BF16),
            room((3, batches, tok, wide), BF16),
            room((batches, 2, tok, wide), BF16),
            room((2, 2, batches, tok, 2 * capacity), BF16),
            room((batches, tok, 1), F32),
            sem((3,)), sem((3,)),
            sem((3,)), sem((3,)),
            sem, sem((batches,)),
            sem, sem,
            sem, sem((CHUNKS,)),
            sem, sem, sem((CHUNKS,)),
            sem, sem((batches, 2)),
            sem, sem((batches, 2)),
            sem, sem((batches, 2, 2)),
            sem, sem((batches, 2)),
            sem, sem((batches, 2)),
            sem, sem((batches,)),
            sem, sem((batches, CHUNKS)),
            sem, sem((batches, CHUNKS)),
            sem((2 + batches,)),
        ],
        compiler_params=pltpu.CompilerParams(
            collective_id=1, has_side_effects=True, vmem_limit_bytes=56 * 2**20
        ),
    )(expert_ids[0], norm_gain, gate_values[0], activations[0], up_weight[0], down_weight[0])
    return received[None]


def local(pipes, *arrays):
    if lax.axis_size("expert") == 2 * GROUP:
        return paired(pipes, *arrays)
    return general(pipes, *arrays)


def solution(mesh):
    placed = (
        P("pipe", None, "expert", None),
        P("pipe", None, "expert"),
        P("pipe", None, "expert"),
        P("pipe", None),
        P("pipe", None, "expert"),
        P("pipe", "expert", None),
    )
    return jax.shard_map(
        functools.partial(local, mesh.shape["pipe"]),
        mesh=mesh,
        in_specs=placed,
        out_specs=P("pipe", None, "expert", None),
        check_vma=False,
    )
```

```python
import functools

import jax
import jax.numpy as jnp
from jax import lax
from jax.experimental import pallas as pl
from jax.experimental.pallas import tpu as pltpu
from jax.sharding import PartitionSpec as P

LEVELS = 2


EPSILON = 1e-06
GROUP = 2**LEVELS
MESH = pl.DeviceIdType.MESH
F32, BF16 = jnp.float32, jnp.bfloat16


def remote(source, target, send, recv, **where):
    return pltpu.make_async_remote_copy(
        src_ref=source, dst_ref=target, send_sem=send, recv_sem=recv, device_id=where, device_id_type=MESH
    )


def each(low, high, body):
    def step(index, carry):
        body(index)
        return carry

    lax.fori_loop(low, high, step, 0)


def layer_kernel(
    n, pipes, place, act, gain, gate, up, down, ret, act_out, place_out, gate_out,
    packed, x, up_all, down_all, pres, sums, own_pre, hidden, out,
    usend, urecv, dsend, drecv, psend, precv, xsend, xrecv, ssend, srecv, hsend, hrecv, rsend, rrecv, own,
):
    me, pipe = lax.axis_index("expert"), lax.axis_index("pipe")
    group_index = me // GROUP
    first = group_index * GROUP
    g = me - first
    batches, experts, capacity = place.shape[:3]
    part, units = up.shape[1:]
    ahead, behind = (pipe + 1) % pipes, (pipe + pipes - 1) % pipes
    blocks = n // GROUP
    tall = GROUP * capacity

    barrier = pltpu.get_barrier_semaphore()

    def greet(k):
        pl.semaphore_signal(barrier, inc=1, device_id={"expert": (me + k) % n}, device_id_type=MESH)

    def greet_behind(k):
        pl.semaphore_signal(barrier, inc=1, device_id={"pipe": behind, "expert": k}, device_id_type=MESH)

    each(1, n, greet)
    each(0, n, greet_behind)
    pl.semaphore_wait(barrier, 2 * n - 1)

    def columns(j):
        return pl.ds(pl.multiple_of(j * part, 128), part)

    def share(j):
        return pl.ds(pl.multiple_of(j * units, 128), units)

    def rows_of(d):
        return pl.ds(pl.multiple_of(d * capacity, 16), capacity)

    peers = [(k, (g + k) % GROUP) for k in range(1, GROUP)]
    ups = [remote(up.at[j], up_all.at[g], usend.at[k], urecv.at[k], expert=first + j) for k, j in peers]
    downs = [
        remote(
            down.at[:, columns(j)], down_all.at[share(g), :], dsend.at[k], drecv.at[k], expert=first + j
        )
        for k, j in peers
    ]
    shifts = [
        remote(source, target, psend.at[i], precv.at[i], pipe=ahead)
        for i, (source, target) in enumerate(((act, act_out), (place, place_out), (gate, gate_out)))
    ]

    def dispatch(m, k):
        d = (me + k) % n
        return remote(packed.at[m, d], x.at[m, rows_of(me), :], xsend.at[m, k], xrecv.at[m, k], expert=d)

    for copy in ups:
        copy.start()
    own_up = pltpu.make_async_copy(up.at[g], up_all.at[g], own.at[0])
    own_down = pltpu.make_async_copy(down.at[:, columns(g)], down_all.at[share(g), :], own.at[1])
    own_up.start()
    own_down.start()
    own_rows = []
    for m in range(batches):
        wide = act[m].astype(F32)
        scale = lax.rsqrt(jnp.mean(wide * wide, axis=-1, keepdims=True) + EPSILON)
        normed = (wide * scale * gain[...].astype(F32)).astype(BF16)
        for e in range(experts):
            for j in range(GROUP):
                packed[m, e * GROUP + j] = jnp.dot(
                    place[m, e], normed[:, j * part : (j + 1) * part], preferred_element_type=F32
                ).astype(BF16)
        if m == 0:
            each(1, n, lambda k: dispatch(0, k).start())
        copy = pltpu.make_async_copy(packed.at[m, me], x.at[m, rows_of(me), :], own.at[2 + m])
        copy.start()
        own_rows.append(copy)

    def summing(m, k, j):
        return remote(pres.at[m, k], sums.at[m, k], ssend.at[m, k], srecv.at[m, k], expert=first + j)

    def sharing(m, k, j):
        mine = hidden.at[m, :, share(g)]
        return remote(mine, mine, hsend.at[m, k], hrecv.at[m, k], expert=first + j)

    own_up.wait()
    for copy in ups:
        copy.wait_recv()
    for m in range(batches):
        own_rows[m].wait()
        each(1, n, lambda k, m=m: dispatch(m, k).wait_recv())
        for k, j in peers:
            pres[m, k] = jnp.dot(x[m], up_all[j], preferred_element_type=F32).astype(BF16)
            summing(m, k, j).start()
        if m + 1 < batches:
            each(1, n, lambda k, m=m: dispatch(m + 1, k).start())
        if m == 0:
            for copy in downs + shifts:
                copy.start()
        own_pre[...] = jnp.dot(x[m], up_all[g], preferred_element_type=F32)
        for k, j in peers:
            summing(m, k, j).wait_recv()
        total = own_pre[...]
        for k in range(1, GROUP):
            total = total + sums[m, k].astype(F32)
        hidden[m, :, share(g)] = jax.nn.silu(total).astype(BF16)
        for k, j in peers:
            sharing(m, k, j).start()

    def slots_of(m, source):
        return ret.at[m, rows_of(source // GROUP), columns(source % GROUP)]

    def give(m, target):
        return remote(
            out.at[m, rows_of(target), :], slots_of(m, me), rsend.at[m, target], rrecv.at[m, me],
            pipe=ahead, expert=target,
        )

    own_down.wait()
    for copy in downs:
        copy.wait_recv()
    for m in range(batches):
        for k, j in peers:
            sharing(m, k, j).wait_recv()

        def block(index, m=m):
            owner = (group_index + 1 + index) % blocks
            rows = pl.ds(pl.multiple_of(owner * tall, 16), tall)
            out[m, rows, :] = jnp.dot(
                hidden[m, rows, :], down_all[...], preferred_element_type=F32
            ).astype(BF16)
            for j in range(GROUP):
                give(m, owner * GROUP + j).start()

        each(0, blocks, block)

    for copy in ups + downs:
        copy.wait_send()
    for copy in shifts:
        copy.wait()
    for m in range(batches):
        each(1, n, lambda k, m=m: dispatch(m, k).wait_send())
        for k, j in peers:
            summing(m, k, j).wait_send()
            sharing(m, k, j).wait_send()

        def finish(source, m=m):
            give(m, source).wait_send()
            remote(
                out.at[m, rows_of(source), :], slots_of(m, source), rsend.at[m, source],
                rrecv.at[m, source], pipe=ahead, expert=source,
            ).wait_recv()

        each(0, n, finish)


def general(pipes, activations, expert_ids, gate_values, norm_gain, up_weight, down_weight):
    n = lax.axis_size("expert")
    experts = n // GROUP
    _, batches, tok, width = activations.shape
    part = width // GROUP
    units = up_weight.shape[2]
    capacity = max(2, 3 * tok // (2 * experts))
    capacity = (capacity + 15) // 16 * 16
    rows = n * capacity

    order = jnp.arange(tok, dtype=jnp.int32)
    same = expert_ids[0][:, :, None] == expert_ids[0][:, None, :]
    ranking = jnp.sum((same & (order[None, :] < order[:, None])).astype(jnp.int32), axis=-1)
    slot = expert_ids[0] * capacity + ranking
    slots = jnp.arange(experts * capacity, dtype=jnp.int32).reshape(1, experts, capacity, 1)
    place = (slot[:, None, None, :] == slots).astype(BF16)

    vmem, far = pl.BlockSpec(memory_space=pltpu.VMEM), pl.BlockSpec(memory_space=pl.ANY)
    shape, sem = jax.ShapeDtypeStruct, pltpu.SemaphoreType.DMA
    returned, act_prev, place_prev, gate_prev = pl.pallas_call(
        functools.partial(layer_kernel, n, pipes),
        out_shape=(
            shape((batches, experts * capacity, width), BF16),
            shape((batches, tok, width), BF16),
            shape(place.shape, BF16),
            shape((batches, tok), F32),
        ),
        in_specs=[vmem] * 4 + [far] * 2,
        out_specs=(far,) * 4,
        scratch_shapes=[
            pltpu.VMEM((batches, n, capacity, part), BF16),
            pltpu.VMEM((batches, rows, part), BF16),
            pltpu.VMEM((GROUP, part, units), BF16),
            pltpu.VMEM((GROUP * units, part), BF16),
            pltpu.VMEM((batches, GROUP, rows, units), BF16),
            pltpu.VMEM((batches, GROUP, rows, units), BF16),
            pltpu.VMEM((rows, units), F32),
            pltpu.VMEM((batches, rows, GROUP * units), BF16),
            pltpu.VMEM((batches, rows, part), BF16),
            sem((GROUP,)),
            sem((GROUP,)),
            sem((GROUP,)),
            sem((GROUP,)),
            sem((3,)),
            sem((3,)),
            sem((batches, n)),
            sem((batches, n)),
            sem((batches, GROUP)),
            sem((batches, GROUP)),
            sem((batches, GROUP)),
            sem((batches, GROUP)),
            sem((batches, n)),
            sem((batches, n)),
            sem((2 + batches,)),
        ],
        compiler_params=pltpu.CompilerParams(
            collective_id=0, has_side_effects=True, vmem_limit_bytes=60 * 2**20
        ),
    )(
        place,
        activations[0],
        norm_gain,
        gate_values[0],
        up_weight[0].reshape(GROUP, part, units),
        down_weight[0],
    )

    finished = []
    for m in range(batches):
        expert_out = lax.dot_general(
            place_prev[m].reshape(experts * capacity, tok),
            returned[m],
            (((0,), (0,)), ((), ())),
            preferred_element_type=F32,
        )
        finished.append((act_prev[m].astype(F32) + gate_prev[m][:, None] * expert_out).astype(BF16))
    return jnp.stack(finished)[None]


SLOTS = 4
CHUNKS = 14
EARLY = 8
FIRST = 6
AHEAD = 2
FAR, NEAR, ALL = (2, 2), (0, 2), (0, 4)


def quad_kernel(
    pipes, ids, gain, gate, source, up, down, out,
    act, ids_all, ids_prev, gate_prev, act_prev, place, dense, halves, x, mixed, wu, wd,
    pre, pre_send, pre_recv, hidden, results, ret, parcels, arrived, spread, gates,
    isend, irecv, ssend, srecv, nsend, nrecv, usend, urecv, dsend, drecv, osend, fsend, frecv,
    gsend, grecv, zsend, zrecv, msend, mrecv, psend, precv, hsend, hrecv, ksend, krecv, rsend, rrecv, esend, erecv, own,
):
    me, pipe = lax.axis_index("expert"), lax.axis_index("pipe")
    z, y = me // 2, me % 2
    other = 1 - y
    half = z // 2
    s = (1 - half) * z + half * (3 - z)
    inner, outer = s == 1, s == 0
    batches, tok, width = act.shape
    wide = width // 2
    units = up.shape[1]
    capacity = x.shape[3]
    rows = 2 * SLOTS * capacity
    part = wide // CHUNKS
    block = 2 * capacity
    ahead, behind = (pipe + 1) % pipes, (pipe + pipes - 1) % pipes

    def node(owner, slot, at):
        return ((1 - at) * slot + at * (3 - slot)) * 2 + owner

    beside, across, corner, mate = node(other, s, half), node(y, 1 - s, half), node(other, 1 - s, half), node(y, 1, 1 - half)

    loads = [pltpu.make_async_copy(source.at[m], act.at[m], own.at[2 + m]) for m in range(batches)]
    for copy in loads:
        copy.start()
    barrier = pltpu.get_barrier_semaphore()

    def greet(**where):
        pl.semaphore_signal(barrier, inc=1, device_id=where, device_id_type=MESH)

    for device in (beside, across, corner):
        greet(expert=device)
    greet(pipe=behind, expert=me)

    @pl.when(inner)
    def _():
        greet(expert=mate)
        greet(pipe=behind, expert=mate)
        pl.semaphore_wait(barrier, 6)

    @pl.when(outer)
    def _():
        pl.semaphore_wait(barrier, 4)

    def wide_half(j):
        return pl.ds(pl.multiple_of(j * wide, 128), wide)

    def span(c):
        return c if isinstance(c, tuple) else (c, c * part, part)

    def double(k):
        return 2 * k, 2 * k * part, 2 * part

    def group_of(c):
        if isinstance(c, tuple):
            return c[0] // 2
        return c - EARLY // 2 if isinstance(c, int) and c > EARLY else c // 2

    def piece(c):
        _, start, size = span(c)
        return pl.ds(pl.multiple_of(start, 128), size)

    def piece_of(j, c):
        _, start, size = span(c)
        return pl.ds(pl.multiple_of(j * wide + start, 128), size)

    def share(j):
        return pl.ds(pl.multiple_of(j * units, 128), units)

    def id_copy(k, device, target):
        return remote(ids, target, isend.at[k], irecv.at[k], expert=device)

    id_out = [id_copy(k, device, ids_all.at[s, y]) for k, device in enumerate((beside, across, corner))]
    id_in = [
        id_copy(0, beside, ids_all.at[s, other]),
        id_copy(1, across, ids_all.at[1 - s, y]),
        id_copy(2, corner, ids_all.at[1 - s, other]),
    ]
    shifts = [
        remote(source, target, ssend.at[i], srecv.at[i], pipe=ahead)
        for i, (source, target) in enumerate(((ids_all, ids_prev), (gate, gate_prev), (source, act_prev)))
    ]

    def swap_rows(m, owner):
        return remote(halves.at[m], dense.at[m, s, owner], nsend, nrecv.at[m], expert=beside)

    def swap_up(j):
        return remote(up.at[wide_half(other), :], wu.at[:, share(j)], usend, urecv, expert=beside)

    def swap_down(c, j):
        return remote(
            down.at[:, piece_of(other, c)], wd.at[s, share(j), piece(c)], dsend, drecv.at[c], expert=beside
        )

    def lift_down(c):
        return remote(
            down.at[:, piece_of(y, c)], wd.at[0, share(y), piece(c)], osend, frecv.at[c], expert=across
        )

    def pass_down(c):
        block = wd.at[0, share(other), piece(c)]
        return remote(block, block, fsend, frecv.at[c], expert=across)

    def lift_rows(m, owner):
        block = dense.at[m, 0, owner]
        return remote(block, block, gsend, grecv.at[m, owner], expert=across)

    def drop_rows(m, owner, slot):
        rows_there = x.at[m, slot, owner]
        return remote(rows_there, rows_there, zsend, zrecv.at[m, slot // 2], expert=across)

    def cross(m, owner, slot):
        return remote(
            mixed.at[m, owner, slot], x.at[m, 2 + slot, owner], msend,
            mrecv.at[m, owner, slot], expert=mate,
        )

    def lines(slot, count):
        return pl.ds(slot * block, count * block)

    def swap_pre(m, slot, count):
        return remote(
            pre_send.at[m, lines(slot, count)], pre_recv.at[m, lines(slot, count)], psend,
            precv.at[m, slot // 2], expert=beside,
        )

    def lift_hidden(m, slot, count):
        if slot:
            there = hidden.at[m, 0, pl.ds(slot, count)]
            return remote(there, there, hsend, hrecv.at[m, 1], expert=across)
        there = hidden.at[m, 0, pl.ds(0, count), y]
        return remote(there, there, ksend, hrecv.at[m, 0], expert=across)

    def share_hidden(m, owner):
        there = hidden.at[m, 0, pl.ds(0, 2), owner]
        return remote(there, there, ksend, krecv.at[m], expert=beside)

    def give(m, c, far):
        where = {"pipe": ahead, "expert": mate if far else me}
        return remote(
            results.at[m, pl.ds(far * SLOTS, SLOTS), :, piece(c)], ret.at[m, :, half, :, piece(c)],
            rsend, rrecv.at[m, group_of(c)], **where,
        )

    def taken(m, c):
        both = ret.at[m, :, :, :, piece(c)]
        return remote(both, both, rsend, rrecv.at[m, group_of(c)], pipe=ahead)

    targets = ((0, other, corner), (0, y, across), (1, other, beside))

    def deliver(m, c, k):
        return remote(
            parcels.at[k, m, :, piece(c)], arrived.at[m, y, :, piece(c)], esend, erecv.at[m, group_of(c)],
            expert=targets[k][2],
        )

    def delivered(there, m, c):
        return remote(there, there, esend, erecv.at[m, group_of(c)], expert=beside)

    own_up = pltpu.make_async_copy(up.at[wide_half(y), :], wu.at[:, share(y)], own.at[0])
    own_down = pltpu.make_async_copy(down.at[:, wide_half(y)], wd.at[1, share(y), :], own.at[1])

    for copy in id_out:
        copy.start()
    own_up.start()

    def normalise(m):
        loads[m].wait()
        mine = act[m, :, wide_half(y)].astype(F32)
        far = act[m, :, wide_half(other)].astype(F32)
        total = jnp.sum(mine * mine, axis=-1, keepdims=True) + jnp.sum(far * far, axis=-1, keepdims=True)
        scale = lax.rsqrt(total / width + EPSILON)
        halves[m] = (far * scale * gain[:, wide_half(other)].astype(F32)).astype(BF16)
        swap_rows(m, y).start()
        dense[m, s, y] = (mine * scale * gain[:, wide_half(y)].astype(F32)).astype(BF16)

    normalise(0)

    @pl.when(outer)
    def _():
        lift_rows(0, y).start()
        lift_down(0).start()

    lane = lax.broadcasted_iota(jnp.int32, (tok, tok), 1)
    line = lax.broadcasted_iota(jnp.int32, (tok, tok), 0)
    earlier = (line < lane).astype(BF16)
    later = (lane < line).astype(BF16)
    same = lane == line
    slot_line = lax.broadcasted_iota(jnp.int32, (capacity, tok), 0).astype(F32)
    slot_lane = lax.broadcasted_iota(jnp.int32, (tok, block), 1).astype(F32)
    expert_line = lax.broadcasted_iota(jnp.int32, (16, tok), 0)
    expert_lane = lax.broadcasted_iota(jnp.int32, (tok, 128), 1).astype(F32)

    def plan(slot, owner, m):
        onehot = (ids_all[slot, owner, m : m + 1, :] == expert_line).astype(F32)
        before = jnp.dot(onehot.astype(BF16), earlier, preferred_element_type=F32)
        for e in range(2):
            hit = jnp.where(before[e : e + 1] == slot_line, onehot[e : e + 1], 0.0)
            place[slot, owner, m, e] = hit.astype(BF16)

    def plan_back(slot, owner, m):
        line_ids = ids_prev[slot, owner, m : m + 1, :].astype(F32)
        chosen = jnp.sum(jnp.where(same, line_ids, 0.0), axis=1, keepdims=True)
        onehot = (chosen == expert_lane).astype(F32)
        before = jnp.dot(later, onehot.astype(BF16), preferred_element_type=F32)
        rank = jnp.sum(before * onehot, axis=1, keepdims=True)
        spread[slot, owner, m] = (chosen * capacity + rank == slot_lane).astype(BF16)

    ids_all[s, y] = ids[...]
    plan(s, y, 0)

    def pack(m, slot, owner, expert):
        return jnp.dot(
            place[slot, owner, m, expert], dense[m, slot, owner], preferred_element_type=F32
        ).astype(BF16)

    def keep(m, slot, owner):
        x[m, slot, owner] = pack(m, slot, owner, half)

    def pack_cross(m, slot, owner):
        mixed[m, owner, slot] = pack(m, slot, owner, 1 - half)
        cross(m, owner, slot).start()

    def pack_inner(m, owner):
        keep(m, 1, owner)
        drop_rows(m, owner, 1).start()
        pack_cross(m, 1, owner)

    def lifted(m, owner):
        lift_rows(m, owner).wait_recv()
        pack_cross(m, 0, owner)
        keep(m, 0, owner)

    def plan_others():
        for copy in id_in:
            copy.wait_recv()
        for copy in shifts:
            copy.start()
        plan(s, y, 1)
        for m in range(batches):
            plan(s, other, m)

    def forward(m, owner, slot):
        cross(m, owner, slot - 2).wait_recv()
        drop_rows(m, owner, slot).start()

    def partial(m, slot, count):
        total = jnp.dot(
            x[m, slot : slot + count].reshape(count * block, wide), wu[...], preferred_element_type=F32
        )
        pre_send[m, lines(slot, count)] = total.astype(BF16)
        swap_pre(m, slot, count).start()
        pre[m, lines(slot, count)] = total

    def activate(m, slot, count):
        swap_pre(m, slot, count).wait_recv()
        there = lines(slot, count)
        value = jax.nn.silu(pre[m, there] + pre_recv[m, there].astype(F32)).astype(BF16)
        hidden[m, s, pl.ds(slot, count)] = value.reshape(count, 2, capacity, 2 * units)

    @pl.when(inner)
    def _():
        pack_inner(0, y)
        normalise(1)
        own_down.start()
        plan_others()
        for owner in (y, other):
            for m in range(batches):
                plan(0, owner, m)
        swap_rows(0, other).wait_recv()
        swap_up(y).start()
        swap_down(0, y).start()
        pack_inner(0, other)
        lifted(0, y)
        forward(0, y, 3)
        forward(0, other, 3)
        lifted(0, other)
        pack_cross(1, 1, y)
        swap_rows(1, other).wait_recv()
        pack_cross(1, 1, other)
        forward(0, y, 2)
        lifted(1, y)
        forward(0, other, 2)
        for owner in (y, other):
            keep(1, 1, owner)
        shifts[0].wait_recv()
        for m in range(batches):
            plan_back(0, y, m)
            plan_back(0, other, m)
        lifted(1, other)
        forward(1, y, 3)
        for m in range(batches):
            plan_back(1, y, m)
            plan_back(1, other, m)
        forward(1, other, 3)
        own_up.wait()
        forward(1, y, 2)
        swap_up(other).wait_recv()
        partial(0, *FAR)
        each(1, FIRST, lambda c: swap_down(c, y).start())
        forward(1, other, 2)
        for owner in (y, other):
            drop_rows(1, owner, 1).start()
        partial(1, *FAR)
        partial(0, *NEAR)
        swap_down(FIRST, y).start()
        own_down.wait()

    @pl.when(outer)
    def _():
        normalise(1)
        plan_others()
        keep(0, 0, y)
        keep(1, 0, y)
        swap_rows(0, other).wait_recv()
        swap_up(y).start()
        swap_down(0, y).start()
        lift_rows(0, other).start()
        lift_rows(1, y).start()
        keep(0, 0, other)
        swap_rows(1, other).wait_recv()
        lift_rows(1, other).start()
        each(1, EARLY + 1, lambda c: lift_down(c).start())
        keep(1, 0, other)
        shifts[0].wait_recv()
        own_up.wait()

        def gathered(m, slot, count):
            if slot + count == SLOTS:
                both = x.at[m, pl.ds(2, 2)]
                remote(both, both, zsend, zrecv.at[m, 1], expert=across).wait_recv()
            if slot == 0:
                remote(x.at[m, 1], x.at[m, 1], zsend, zrecv.at[m, 0], expert=across).wait_recv()

        def relay(c):
            swap_down(c, other).wait_recv()
            pass_down(c).start()

        def relay_next(c):
            relay(c)
            swap_down(c + AHEAD, y).start()

        def late(c):
            lift_down(c + 1).start()
            relay_next(c)


        def raise_hidden(m, slot, count):
            activate(m, slot, count)
            lift_hidden(m, slot, count).start()

        gathered(0, *ALL)
        swap_up(other).wait_recv()
        partial(0, *FAR)
        each(1, 1 + AHEAD, lambda c: swap_down(c, y).start())
        relay(0)
        raise_hidden(0, *FAR)
        each(1, FIRST - AHEAD, relay_next)
        relay(FIRST - AHEAD)
        gathered(1, *FAR)
        partial(1, *FAR)
        partial(0, *NEAR)
        swap_down(FIRST, y).start()
        relay_next(FIRST - 1)
        raise_hidden(1, *FAR)
        raise_hidden(0, *NEAR)
        relay(FIRST)
        gathered(1, *NEAR)
        partial(1, *NEAR)
        swap_down(FIRST + AHEAD, y).start()
        relay_next(FIRST + 1)
        raise_hidden(1, *NEAR)
        each(EARLY, CHUNKS - AHEAD, late)
        lift_down(CHUNKS - 1).start()
        each(CHUNKS - AHEAD, CHUNKS, relay)

    for copy in shifts[1:]:
        copy.wait_recv()
    for m in range(batches):
        gates[m] = jnp.sum(jnp.where(same, gate_prev[m : m + 1, :], 0.0), axis=1, keepdims=True)

    def await_hidden(m, slot, count):
        activate(m, slot, count)
        lift_hidden(m, slot, count).wait_recv()
        if slot == 0:
            share_hidden(m, y).start()

    def await_down(c):
        swap_down(c, other).wait_recv()
        both = wd.at[0, :, piece(c)]
        remote(both, both, fsend, frecv.at[c], expert=across).wait_recv()

    def produce(m, c, slot, count):
        def of(side):
            there = hidden[m, side, pl.ds(slot, count)].reshape(count * block, 2 * units)
            return jnp.dot(there, wd[side, :, piece(c)], preferred_element_type=F32)

        total = of(0) + of(1)
        results[m, pl.ds(2 * slot, 2 * count), :, piece(c)] = total.astype(BF16).reshape(2 * count, capacity, part)
        if slot + count == SLOTS:
            give(m, c, 1).start()
        if slot == 0:
            give(m, c, 0).start()

    def combine(m, c):
        size = span(c)[2]
        taken(m, c).wait_recv()

        def rows_for(slot, owner):
            there = ret[m, 2 * slot + owner, :, :, piece(c)].reshape(block, size)
            return jnp.dot(spread[slot, owner, m], there, preferred_element_type=F32).astype(BF16)

        for k, (slot, owner, _) in enumerate(targets):
            parcels[k, m, :, piece(c)] = rows_for(slot, owner)
            deliver(m, c, k).start()
        arrived[m, y, :, piece(c)] = rows_for(1, y)

    def complete(m, c, j):
        columns = piece_of(j, c)
        out[m, :, columns] = (
            act_prev[m, :, columns].astype(F32) + gates[m] * arrived[m, j, :, piece(c)].astype(F32)
        ).astype(BF16)

    def finish(m, c):
        complete(m, c, y)
        delivered(arrived.at[m, other, :, piece(c)], m, c).wait_recv()
        complete(m, c, other)

    def finish_outer(m, c):
        delivered(arrived.at[m, :, :, piece(c)], m, c).wait_recv()
        for j in range(2):
            complete(m, c, j)

    @pl.when(inner)
    def _():
        def close(c):
            for m in range(batches):
                finish(m, c)

        def join(c):
            for m in range(batches):
                combine(m, c)

        def first(c):
            await_down(c)
            produce(0, c, *FAR)

        def third(c):
            await_down(c)
            produce(0, c, *ALL)
            produce(1, c, *FAR)

        def late(c):
            await_down(c)
            produce(0, c, *ALL)
            produce(1, c, *ALL)

        await_hidden(0, *FAR)
        each(0, FIRST, first)
        await_hidden(1, *FAR)
        each(0, FIRST, lambda c: produce(1, c, *FAR))
        await_hidden(0, *NEAR)
        swap_down(FIRST + 1, y).start()
        partial(1, *NEAR)
        swap_down(EARLY, y).start()
        share_hidden(0, other).wait_recv()
        each(0, FIRST, lambda c: produce(0, c, *NEAR))
        third(FIRST)
        third(FIRST + 1)
        combine(0, double(0))
        combine(0, double(1))
        await_hidden(1, *NEAR)
        each(EARLY + 1, CHUNKS, lambda c: swap_down(c, y).start())
        third(EARLY)
        combine(0, double(2))
        share_hidden(1, other).wait_recv()
        each(0, EARLY + 1, lambda c: produce(1, c, *NEAR))
        combine(1, double(0))
        late(EARLY + 1)
        each(1, 3, lambda k: combine(1, double(k)))
        join(double(3))
        late(EARLY + 2)
        join(EARLY)
        close(double(0))
        late(EARLY + 3)
        join(EARLY + 1)
        close(double(1))
        late(EARLY + 4)
        join(EARLY + 2)
        close(double(2))
        late(EARLY + 5)
        close(double(3))
        join(EARLY + 3)
        close(EARLY)
        join(EARLY + 4)
        for c in range(EARLY + 1, EARLY + 4):
            close(c)
        join(EARLY + 5)
        for c in range(EARLY + 4, CHUNKS):
            close(c)

    @pl.when(outer)
    def _():
        for m in range(batches):
            each(0, EARLY // 2, lambda k, m=m: finish_outer(m, double(k)))

        def rest(c):
            for m in range(batches):
                finish_outer(m, c)

        for c in range(EARLY, CHUNKS):
            rest(c)

    for copy in id_out + shifts:
        copy.wait_send()
    swap_up(y).wait_send()
    remote(down.at[:, wide_half(other)], wd.at[s, share(y), :], dsend, drecv.at[0], expert=beside).wait_send()

    def all_sent(whole, sent):
        remote(whole, whole, sent, frecv.at[0], expert=beside).wait_send()

    all_sent(halves, nsend)
    all_sent(hidden.at[:, 0, pl.ds(0, 2), y], ksend)
    all_sent(pre_send, psend)

    @pl.when(inner)
    def _():
        all_sent(x.at[:, pl.ds(1, 3)], zsend)
        all_sent(mixed, msend)
        all_sent(results, rsend)
        all_sent(parcels, esend)

    @pl.when(outer)
    def _():
        all_sent(hidden.at[:, 0, pl.ds(2, 2)], hsend)
        all_sent(dense.at[:, 0], gsend)
        moved = wd.at[0, share(y), :]
        all_sent(moved, osend)
        all_sent(moved, fsend)


def paired(pipes, activations, expert_ids, gate_values, norm_gain, up_weight, down_weight):
    _, batches, tok, width = activations.shape
    wide = width // 2
    units = up_weight.shape[2]
    capacity = (3 * tok // 4 + 15) // 16 * 16
    rows = 2 * SLOTS * capacity
    vmem, far = pl.BlockSpec(memory_space=pltpu.VMEM), pl.BlockSpec(memory_space=pl.ANY)
    room, sem = pltpu.VMEM, pltpu.SemaphoreType.DMA
    received = pl.pallas_call(
        functools.partial(quad_kernel, pipes),
        out_shape=pltpu.VMEM((batches, tok, width), BF16),
        in_specs=[vmem] * 3 + [far] * 3,
        out_specs=vmem,
        scratch_shapes=[
            room((batches, tok, width), BF16),
            room((2, 2, batches, tok), jnp.int32),
            room((2, 2, batches, tok), jnp.int32),
            room((batches, tok), F32),
            room((batches, tok, width), BF16),
            room((2, 2, batches, 2, capacity, tok), BF16),
            room((batches, 2, 2, tok, wide), BF16),
            room((batches, tok, wide), BF16),
            room((batches, SLOTS, 2, capacity, wide), BF16),
            room((batches, 2, 2, capacity, wide), BF16),
            room((wide, 2 * units), BF16),
            room((2, 2 * units, wide), BF16),
            room((batches, rows, 2 * units), F32),
            room((batches, rows, 2 * units), BF16),
            room((batches, rows, 2 * units), BF16),
            room((batches, 2, SLOTS, 2, capacity, 2 * units), BF16),
            room((batches, 2 * SLOTS, capacity, wide), BF16),
            room((batches, SLOTS, 2, capacity, wide), BF16),
            room((3, batches, tok, wide), BF16),
            room((batches, 2, tok, wide), BF16),
            room((2, 2, batches, tok, 2 * capacity), BF16),
            room((batches, tok, 1), F32),
            sem((3,)), sem((3,)),
            sem((3,)), sem((3,)),
            sem, sem((batches,)),
            sem, sem,
            sem, sem((CHUNKS,)),
            sem, sem, sem((CHUNKS,)),
            sem, sem((batches, 2)),
            sem, sem((batches, 2)),
            sem, sem((batches, 2, 2)),
            sem, sem((batches, 2)),
            sem, sem((batches, 2)),
            sem, sem((batches,)),
            sem, sem((batches, CHUNKS - EARLY // 2)),
            sem, sem((batches, CHUNKS - EARLY // 2)),
            sem((2 + batches,)),
        ],
        compiler_params=pltpu.CompilerParams(
            collective_id=1, has_side_effects=True, vmem_limit_bytes=56 * 2**20
        ),
    )(expert_ids[0], norm_gain, gate_values[0], activations[0], up_weight[0], down_weight[0])
    return received[None]


def local(pipes, *arrays):
    if lax.axis_size("expert") == 2 * GROUP:
        return paired(pipes, *arrays)
    return general(pipes, *arrays)


def solution(mesh):
    placed = (
        P("pipe", None, "expert", None),
        P("pipe", None, "expert"),
        P("pipe", None, "expert"),
        P("pipe", None),
        P("pipe", None, "expert"),
        P("pipe", "expert", None),
    )
    return jax.shard_map(
        functools.partial(local, mesh.shape["pipe"]),
        mesh=mesh,
        in_specs=placed,
        out_specs=P("pipe", None, "expert", None),
        check_vma=False,
    )
```
